256 devices in a mesh: pair: 32 (over z, x), occ: 8 (over y, core).
Axes of the slice: x: 4, y: 4, z: 8, core: 2. Of those that a mesh axis runs over, the one named last changes fastest.
Arguments:
- integrals: bfloat16 [32, 256, 64, 1024], P('pair', None, None, 'occ'), may hold values from -6 to 6
- occ_coeffs: bfloat16 [6144, 128], replicated, may hold values from -0.125 to 0.125
- virt_coeffs: bfloat16 [6144, 5120], P(None, 'pair'), may hold values from -0.078125 to 0.078125
- block_ids: int32 [2, 32, 256], P(None, 'pair'), may hold values from 0 to 95, as said below
- live_mask: int32 [32, 256], P('pair'), may hold values from 0 to 1, as said below
Outputs:
- factors: bfloat16 [128, 16, 5120], P('occ', None, 'pair')
The draws below stay inside these ranges and needn't reach their ends.
Inputs may be any that keep to these rules, and one draw needn't show every extreme that they name: `block_ids`: slot s of pair index p holds a nu block N with N // 3 == s // 8; each (mu block, nu block) pair is held by at most one slot of all pair indices. `live_mask`: among the 8 slots s with the same s // 8 of one pair index, at most 4 are 1, and exactly 4 for some such group of every pair index.
All inputs are finite; a program needn't handle non-finite values.
Results may differ from the reference program's by a relative error of at most 0.017.
Values may be sent and summed in bfloat16 or wider, within the bound.
A program may use at most 64 MiB of HBM per device.

```python
import jax
import jax.numpy as jnp
from jax import lax

NB = 96
BS = 64
NBF = 6144
AUX = 16
OB = 128
NV = 5120
GROUP = 8
LIVE = 4
SLOTS = 256
N_PAIR = 32


def block_table(base_key):
    owned_count = NB // N_PAIR

    def per_owner(owner_index):
        ranking = jax.random.permutation(jax.random.fold_in(base_key, owner_index), owned_count * NB)
        ranking = ranking[:GROUP * N_PAIR]
        mu_part = ranking // owned_count
        nu_part = owner_index * owned_count + ranking % owned_count
        return jnp.stack([mu_part, nu_part]).reshape(2, N_PAIR, GROUP)
    table = jax.vmap(per_owner)(jnp.arange(N_PAIR))
    return jnp.transpose(table, (1, 2, 0, 3)).reshape(2, N_PAIR, N_PAIR * GROUP).astype(jnp.int32)


def draw_block_ids(key, part):
    return block_table(jax.random.fold_in(key, 11))


def draw_live_mask(key, part):
    count_key, rank_key = jax.random.split(jax.random.fold_in(key, 23))
    counts = jax.random.randint(count_key, (N_PAIR, N_PAIR), 1, LIVE + 1)
    diagonal = jnp.arange(N_PAIR)[:, None] == jnp.arange(N_PAIR)[None, :]
    counts = jnp.where(diagonal, LIVE, counts)
    scores = jax.random.randint(rank_key, (N_PAIR, N_PAIR, GROUP), 0, 1 << 20) * GROUP + jnp.arange(GROUP)
    rank_table = jnp.argsort(jnp.argsort(scores, axis=2), axis=2)
    flags = (rank_table < counts[:, :, None]).astype(jnp.int32)
    return flags.reshape(N_PAIR, N_PAIR * GROUP)


def levels(stream_key, dims, cuts, least, top_value):
    level = 1.0
    for axis_at, parts in cuts:
        heights = jax.random.uniform(jax.random.fold_in(jax.random.fold_in(stream_key, 6), axis_at), (parts,), jnp.float32, least / len(cuts), top_value / len(cuts))
        level = level * jnp.repeat(jnp.exp(heights), dims[axis_at] // parts).reshape((-1,) + (1,) * (len(dims) - 1 - axis_at))
    return level


def gaussian(own_key, extent, scale, most, cuts=(), kind=jnp.bfloat16):
    level = levels(own_key, extent, cuts, -0.22, 0.18) if cuts else 1.0
    values = jax.random.normal(own_key, extent, jnp.float32) * scale * level
    return jnp.minimum(jnp.maximum(values, -most), most).astype(kind)


def setup_inputs(seed: int = 0) -> dict:
    key_of = jax.random.split(jax.random.key(seed), 6)
    integrals = gaussian(key_of[0], (N_PAIR, SLOTS, BS, AUX * BS), 1.0, 6.0, ((0, 32), (3, 8)))
    occ_coeffs = gaussian(key_of[1], (NBF, OB), (32 * BS) ** -0.5, 0.125)
    virt_coeffs = gaussian(key_of[2], (NBF, NV), NBF ** -0.5, 0.078125, ((1, 32),))
    block_ids = draw_block_ids(jax.random.fold_in(key_of[5], 71), 0)
    live_mask = draw_live_mask(jax.random.fold_in(key_of[5], 71), 0)
    return {"integrals": integrals, "occ_coeffs": occ_coeffs, "virt_coeffs": virt_coeffs, "block_ids": block_ids, "live_mask": live_mask}


def reference(integrals, occ_coeffs, virt_coeffs, block_ids, live_mask):
    coeff_blocks = occ_coeffs.astype(jnp.float32).reshape(NB, BS, OB)

    def scan_step(running, inputs):
        block_data, mu_index, nu_index, live_flags = inputs
        coeff_rows = coeff_blocks[mu_index]
        shaped = block_data.astype(jnp.float32).reshape(SLOTS, BS, AUX, BS)
        partial_terms = jnp.einsum("snqm,smi->snqi", shaped, coeff_rows, precision=lax.Precision.HIGHEST)
        partial_terms = partial_terms * live_flags.astype(jnp.float32)[:, None, None, None]
        return running.at[nu_index].add(partial_terms), None

    start_sums = jnp.zeros((NB, BS, AUX, OB), jnp.float32)
    running, _ = lax.scan(scan_step, start_sums, (integrals, block_ids[0], block_ids[1], live_mask))
    half_sums = running.astype(jnp.bfloat16).reshape(NBF, AUX * OB)
    product = jnp.dot(half_sums.T, virt_coeffs, preferred_element_type=jnp.float32)
    return product.reshape(AUX, OB, NV).transpose(1, 0, 2).astype(jnp.bfloat16)
```

```python
import jax
import jax.numpy as jnp
from jax import lax
from jax.experimental import pallas as pl
from jax.experimental.pallas import tpu as pltpu
from jax.sharding import PartitionSpec as P

NZ, NX = 8, 4
OWNERS = NZ * NX
GROUP = 8
OWNED = 3
BS = 64
ROWS = OWNED * BS
CUT = 112
MESH = pl.DeviceIdType.MESH
UP, DOWN = NZ // 2, NZ // 2 - 1


def far_first(k):
    return (NZ // 2 - (k + 1) // 2) * (1 - 2 * (k % 2))


def kernel(
    ids, live, a_hbm, c_hbm, vt_hbm, out,
    a, c, vt, s, h, acc, stage,
    ax2, ax1, axm, bz, bzm, az, azm, bx, bxm,
    ax2_s, ax1_s, axm_s, bz_s, bzm_s, az_s, azm_s, bx_s, bxm_s,
    gaz_s, gazm_s, gax0_s, gax1_s, gaxm_s, gbx_s, gbxm_s, gbz_s, gbzm_s,
    occ_s, in_s,
):
    me, o = lax.axis_index("pair"), lax.axis_index("occ")
    n_occ = lax.axis_size("occ")
    z, x = me // NX, me % NX
    m = 1 - 2 * (o % 2)
    rows_a, rows_b = pl.ds(0, CUT), pl.ds(CUT, ROWS - CUT)

    def zat(d):
        return (z + d * m + NZ) % NZ

    def xat(d):
        return (x + d * m + NX) % NX

    z_up, z_down = zat(1) * NX + x, zat(-1) * NX + x
    x_up, x_down = z * NX + xat(1), z * NX + xat(-1)

    def copy(src, dst, sems, k, to):
        return pltpu.make_async_remote_copy(
            src_ref=src, dst_ref=dst, send_sem=sems.at[0, k], recv_sem=sems.at[1, k],
            device_id={"pair": to}, device_id_type=MESH,
        )

    def load_a(k):
        at = pl.ds(zat(far_first(k)) * NX * GROUP, NX * GROUP)
        return pltpu.make_async_copy(a_hbm.at[at], a.at[at], in_s.at[k])

    load_c = pltpu.make_async_copy(c_hbm, c.at[pl.ds(0, NZ * NX * OWNED)], in_s.at[NZ])
    load_v = pltpu.make_async_copy(vt_hbm, vt, in_s.at[NZ + 1])
    load_c.start()

    @pl.loop(0, NZ)
    def _(k):
        load_a(k).start()

    load_v.start()

    barrier = pltpu.get_barrier_semaphore()
    for to in (z_up, z_down, x_up, x_down):
        pl.semaphore_signal(barrier, inc=1, device_id={"pair": to}, device_id_type=MESH)
    for d in range(1, n_occ):
        pl.semaphore_signal(
            barrier, inc=1, device_id={"occ": (o + d) % n_occ}, device_id_type=MESH
        )
    c[NZ * NX * OWNED] = jnp.zeros((BS, c.shape[2]), c.dtype)
    load_c.wait()

    def ax2_copy(k):
        zz = zat(far_first(k))
        return copy(s.at[zz, xat(2), rows_a], ax2.at[k], ax2_s, k, x_up)

    def ax1_copy(k):
        zz = zat(far_first(k))
        return copy(s.at[zz, xat(1), rows_a], ax1.at[k], ax1_s, k, x_up)

    def axm_copy(k):
        zz = zat(far_first(k))
        return copy(s.at[zz, xat(-1), rows_a], axm.at[k], axm_s, k, x_down)

    def bz_copy(t):
        return copy(s.at[zat(UP - t), :, rows_b], bz.at[t], bz_s, t, z_up)

    def bzm_copy(t):
        return copy(s.at[zat(t - DOWN), :, rows_b], bzm.at[t], bzm_s, t, z_down)

    def az_copy(t):
        return copy(s.at[zat(UP - t), x, rows_a], az.at[t], az_s, t, z_up)

    def azm_copy(t):
        return copy(s.at[zat(t - DOWN), x, rows_a], azm.at[t], azm_s, t, z_down)

    def bx_copy(t):
        return copy(s.at[z, xat(2 - t), rows_b], bx.at[t], bx_s, t, x_up)

    bxm_copy = copy(s.at[z, xat(-1), rows_b], bxm, bxm_s, 0, x_down)

    def add(at, *terms):
        total = s[at].astype(jnp.float32)
        for t in terms:
            total += t.astype(jnp.float32)
        s[at] = total.astype(s.dtype)

    def transform(zz, xx):
        q = zz * NX + xx
        left, right, picks = [], [], [[] for _ in range(OWNED)]
        for j in range(GROUP // 2):
            even, odd = a[q * GROUP + 2 * j], a[q * GROUP + 2 * j + 1]
            left.append(jnp.concatenate([even[:, :BS], odd[:, :BS]], axis=1))
            right.append(jnp.concatenate([even[:, BS:], odd[:, BS:]], axis=1))
        for j in range(GROUP):
            slot = q * GROUP + j
            mu, nu, on = ids[0, 0, slot], ids[1, 0, slot], live[0, slot]
            for b in range(OWNED):
                hit = jnp.logical_and(on != 0, nu == q * OWNED + b)
                picks[b].append(c[jnp.where(hit, mu, NZ * NX * OWNED)])
        lhs = jnp.concatenate(
            [jnp.concatenate(left, axis=1), jnp.concatenate(right, axis=1)], axis=0
        )
        rhs = jnp.concatenate([jnp.concatenate(p, axis=0) for p in picks], axis=1)
        got = jnp.dot(lhs, rhs, preferred_element_type=jnp.float32).astype(s.dtype)
        n_i = c.shape[2]
        for b in range(OWNED):
            for side in range(2):
                s[zz, xx, pl.ds(b * BS, BS), pl.ds(side * n_i, n_i)] = got[
                    side * BS : (side + 1) * BS, b * n_i : (b + 1) * n_i
                ]

    @pl.loop(0, NZ)
    def _(k):
        zz = zat(far_first(k))
        load_a(k).wait()

        @pl.loop(0, NX)
        def _(xx):
            transform(zz, xx)

        @pl.when(k == 0)
        def _():
            pl.semaphore_wait(barrier, 4 + n_occ - 1)

        ax2_copy(k).start()
        axm_copy(k).start()

        @pl.when(k == 0)
        def _():
            bz_copy(0).start()

        @pl.when(k == 1)
        def _():
            bzm_copy(0).start()

    def bz_step(t):
        bz_copy(t).wait_recv()
        add((zat(UP - 1 - t), slice(None), rows_b), bz[t])
        bz_copy(t + 1).start()

    def bzm_step(t):
        bzm_copy(t).wait_recv()
        add((zat(t + 1 - DOWN), slice(None), rows_b), bzm[t])
        bzm_copy(t + 1).start()

    def az_step(t):
        az_copy(t).wait_recv()
        add((zat(UP - 1 - t), x, rows_a), az[t])
        az_copy(t + 1).start()

    def azm_step(t):
        azm_copy(t).wait_recv()
        add((zat(t + 1 - DOWN), x, rows_a), azm[t])
        azm_copy(t + 1).start()

    def ax_steps(lo, hi):
        @pl.loop(lo, hi)
        def _(k):
            ax2_copy(k).wait_recv()
            add((zat(far_first(k)), xat(1), rows_a), ax2[k])
            ax1_copy(k).start()

    bz_step(0)
    bzm_step(0)
    ax_steps(0, 3)
    bz_step(1)
    bzm_step(1)
    ax_steps(3, 6)
    bz_step(2)
    ax_steps(6, 8)
    bzm_copy(2).wait_recv()
    bz_copy(3).wait_recv()
    add((z, slice(None), rows_b), bz[3], bzm[2])
    bx_copy(0).start()
    bxm_copy.start()

    @pl.loop(0, NZ)
    def _(k):
        ax1_copy(k).wait_recv()
        axm_copy(k).wait_recv()
        add((zat(far_first(k)), x, rows_a), ax1[k], axm[k])

        @pl.when(k == 0)
        def _():
            az_copy(0).start()

        @pl.when(k == 1)
        def _():
            azm_copy(0).start()

    bx_copy(0).wait_recv()
    add((z, xat(1), rows_b), bx[0])
    bx_copy(1).start()
    az_step(0)
    azm_step(0)
    bxm_copy.wait_recv()
    bx_copy(1).wait_recv()

    def gaz_copy(t):
        part = h.at[zat(-t), x, rows_a]
        return copy(part, part, gaz_s, t, z_up)

    def gazm_copy(t):
        part = h.at[zat(t), x, rows_a]
        return copy(part, part, gazm_s, t, z_down)

    def gax0_copy(k):
        part = h.at[zat(far_first(NZ - 1 - k)), x, rows_a]
        return copy(part, part, gax0_s, k, x_up)

    def gax1_copy(k):
        part = h.at[zat(far_first(NZ - 1 - k)), xat(-1), rows_a]
        return copy(part, part, gax1_s, k, x_up)

    def gaxm_copy(k):
        part = h.at[zat(far_first(NZ - 1 - k)), x, rows_a]
        return copy(part, part, gaxm_s, k, x_down)

    def gbx_copy(t):
        part = h.at[z, xat(-t), rows_b]
        return copy(part, part, gbx_s, t, x_up)

    own_b = h.at[z, x, rows_b]
    gbxm_copy = copy(own_b, own_b, gbxm_s, 0, x_down)

    def gbz_copy(t):
        part = h.at[zat(-t), :, rows_b]
        return copy(part, part, gbz_s, t, z_up)

    def gbzm_copy(t):
        part = h.at[zat(t), :, rows_b]
        return copy(part, part, gbzm_s, t, z_down)

    def own(rows, *terms):
        total = s[z, x, rows].astype(jnp.float32)
        for t in terms:
            total += t.astype(jnp.float32)
        h[z, x, rows] = total.astype(h.dtype)

    own(rows_b, bx[1], bxm[...])
    gbx_copy(0).start()
    gbxm_copy.start()
    az_step(1)
    azm_step(1)
    az_step(2)
    gbx_copy(0).wait_recv()
    gbx_copy(1).start()
    gbxm_copy.wait_recv()
    azm_copy(2).wait_recv()
    az_copy(3).wait_recv()
    own(rows_a, az[3], azm[2])
    gaz_copy(0).start()
    gazm_copy(0).start()
    gax0_copy(0).start()
    gaxm_copy(0).start()
    gbx_copy(1).wait_recv()
    gbz_copy(0).start()
    gbzm_copy(0).start()

    @pl.loop(0, NZ)
    def _(k):
        ax2_copy(k).wait_send()
        ax1_copy(k).wait_send()
        axm_copy(k).wait_send()

    for t in range(UP):
        bz_copy(t).wait_send()
        az_copy(t).wait_send()
    for t in range(DOWN):
        bzm_copy(t).wait_send()
        azm_copy(t).wait_send()
    bx_copy(0).wait_send()
    bx_copy(1).wait_send()
    bxm_copy.wait_send()
    load_v.wait()

    def gaz_step(t):
        gaz_copy(t).wait_recv()
        if t + 1 < UP:
            gaz_copy(t + 1).start()
        k = 2 * t + 2 if t + 1 < UP else NZ - 1
        gax0_copy(gather_at(-(t + 1))).start()
        gaxm_copy(gather_at(-(t + 1))).start()
        del k

    def gazm_step(t):
        gazm_copy(t).wait_recv()
        if t + 1 < DOWN:
            gazm_copy(t + 1).start()
        gax0_copy(gather_at(t + 1)).start()
        gaxm_copy(gather_at(t + 1)).start()

    def gather_at(d):
        return [far_first(NZ - 1 - k) % NZ for k in range(NZ)].index(d % NZ)

    def gbz_step(t):
        gbz_copy(t).wait_recv()
        if t + 1 < UP:
            gbz_copy(t + 1).start()

    def gbzm_step(t):
        gbzm_copy(t).wait_recv()
        if t + 1 < DOWN:
            gbzm_copy(t + 1).start()

    def gax_steps(lo, hi):
        @pl.loop(lo, hi)
        def _(k):
            gax0_copy(k).wait_recv()
            gax1_copy(k).start()

    def multiply(k):
        gax1_copy(k).wait_recv()
        gaxm_copy(k).wait_recv()
        zz = zat(far_first(NZ - 1 - k))
        depth = NX * ROWS
        at = pl.ds(pl.multiple_of(zz * depth, 128), depth)
        acc[...] += jnp.dot(
            vt[:, at], h[zz].reshape(depth, h.shape[3]), preferred_element_type=jnp.float32
        )

    acc[...] = jnp.zeros_like(acc)
    gaz_step(0)
    gazm_step(0)
    gax_steps(0, 1)
    gaz_step(1)
    gazm_step(1)
    gbz_step(0)
    gbzm_step(0)
    gaz_step(2)
    gazm_step(2)
    gaz_step(3)
    gax_steps(1, 3)
    gbz_step(1)
    gbzm_step(1)
    gax_steps(3, 5)
    gbz_step(2)
    gbzm_step(2)
    gax_steps(5, 8)

    @pl.loop(0, NZ - 1)
    def _(k):
        multiply(k)

    gbz_step(3)
    multiply(NZ - 1)

    turned = acc[...].T.astype(stage.dtype)
    part = stage.shape[2]
    for side in range(2):
        for d in range(n_occ):
            at = (side * n_occ + d) * part
            stage[d, side] = turned[at : at + part]

    def occ_copy(d):
        return pltpu.make_async_remote_copy(
            src_ref=stage.at[(o + d) % n_occ], dst_ref=out.at[pl.ds(2 * o, 2)],
            send_sem=occ_s.at[0, d], recv_sem=occ_s.at[1, d],
            device_id={"occ": (o + d) % n_occ}, device_id_type=MESH,
        )

    for d in range(1, n_occ):
        occ_copy(d).start()
    mine = pltpu.make_async_copy(stage.at[o], out.at[pl.ds(2 * o, 2)], occ_s.at[0, 0])
    mine.start()

    @pl.loop(0, NZ)
    def _(k):
        gax0_copy(k).wait_send()
        gax1_copy(k).wait_send()
        gaxm_copy(k).wait_send()

    for t in range(UP):
        gaz_copy(t).wait_send()
        gbz_copy(t).wait_send()
    for t in range(DOWN):
        gazm_copy(t).wait_send()
        gbzm_copy(t).wait_send()
    gbx_copy(0).wait_send()
    gbx_copy(1).wait_send()
    gbxm_copy.wait_send()
    mine.wait()
    for d in range(1, n_occ):
        occ_copy(d).wait_send()
        src = (o + n_occ - d) % n_occ
        pltpu.make_async_remote_copy(
            src_ref=stage.at[src], dst_ref=out.at[pl.ds(2 * src, 2)],
            send_sem=occ_s.at[0, d], recv_sem=occ_s.at[1, d],
            device_id={"occ": src}, device_id_type=MESH,
        ).wait_recv()


def on_device(integrals, occ_coeffs, virt_coeffs, block_ids, live_mask):
    blocks = integrals[0]
    n_i = occ_coeffs.shape[1]
    n_a = virt_coeffs.shape[1]
    n_occ = lax.axis_size("occ")
    bf16, f32 = jnp.bfloat16, jnp.float32
    wide = 2 * n_i
    ra, rb = CUT, ROWS - CUT
    any_space, smem = pl.BlockSpec(memory_space=pl.ANY), pl.BlockSpec(memory_space=pltpu.SMEM)

    def sems(k):
        return pltpu.SemaphoreType.DMA((2, k))

    got = pl.pallas_call(
        kernel,
        out_shape=jax.ShapeDtypeStruct((2 * n_occ, n_i // n_occ, n_a), bf16),
        in_specs=[smem, smem, any_space, any_space, any_space],
        out_specs=pl.BlockSpec(memory_space=pltpu.VMEM),
        scratch_shapes=[
            pltpu.VMEM(blocks.shape, bf16),
            pltpu.VMEM((OWNERS * OWNED + 1, BS, n_i), bf16),
            pltpu.VMEM((n_a, OWNERS * ROWS), bf16),
            pltpu.VMEM((NZ, NX, ROWS, wide), bf16),
            pltpu.VMEM((NZ, NX, ROWS, wide), bf16),
            pltpu.VMEM((n_a, wide), f32),
            pltpu.VMEM((n_occ, 2, n_i // n_occ, n_a), bf16),
            pltpu.VMEM((NZ, ra, wide), bf16),
            pltpu.VMEM((NZ, ra, wide), bf16),
            pltpu.VMEM((NZ, ra, wide), bf16),
            pltpu.VMEM((UP, NX, rb, wide), bf16),
            pltpu.VMEM((DOWN, NX, rb, wide), bf16),
            pltpu.VMEM((UP, ra, wide), bf16),
            pltpu.VMEM((DOWN, ra, wide), bf16),
            pltpu.VMEM((2, rb, wide), bf16),
            pltpu.VMEM((rb, wide), bf16),
            sems(NZ), sems(NZ), sems(NZ), sems(UP), sems(DOWN), sems(UP), sems(DOWN), sems(2), sems(1),
            sems(UP), sems(DOWN), sems(NZ), sems(NZ), sems(NZ), sems(2), sems(1), sems(UP), sems(DOWN),
            sems(n_occ),
            pltpu.SemaphoreType.DMA((NZ + 2,)),
        ],
        compiler_params=pltpu.CompilerParams(
            collective_id=0, has_side_effects=True, vmem_limit_bytes=48 << 20
        ),
    )(
        block_ids,
        live_mask,
        blocks,
        occ_coeffs.reshape(OWNERS * OWNED, BS, n_i),
        virt_coeffs.T,
    )
    return jnp.transpose(got, (1, 0, 2))


def solution(mesh):
    return jax.shard_map(
        on_device,
        mesh=mesh,
        in_specs=(
            P("pair", None, None, "occ"),
            P(),
            P(None, "pair"),
            P(None, "pair", None),
            P("pair", None),
        ),
        out_specs=P("occ", None, "pair"),
        check_vma=False,
    )
```

```python
import jax
import jax.numpy as jnp
from jax import lax
from jax.experimental import pallas as pl
from jax.experimental.pallas import tpu as pltpu
from jax.sharding import PartitionSpec as P

NZ, NX = 8, 4
OWNERS = NZ * NX
GROUP = 8
LIVE = 4
OWNED = 3
BS = 64
ROWS = OWNED * BS
CUT = 112
UP, DOWN = NZ // 2, NZ // 2 - 1
MESH = pl.DeviceIdType.MESH
FIRST = ((0, 2), (2, 5), (5, 8))
HALVES = 2

RATE, LATENCY, HOP, WINDOW = 88e3, 1.25, 0.65, 1.5


def far_first(k):
    return (NZ // 2 - (k + 1) // 2) * (1 - 2 * (k % 2))


class Step:
    def __init__(self, name, cost, after, needs, sends, run):
        self.name, self.cost, self.after, self.needs, self.sends, self.run = name, cost, after, needs, sends, run


def in_order(steps):
    by_name = {s.name: s for s in steps}
    maker = {m[0]: (s, m) for s in steps for m in s.sends}
    follow = {s.name: [] for s in steps}
    for s in steps:
        for p in s.after:
            follow[p].append((s.name, 0.0))
        for n in s.needs:
            p, (_, _, size, hops) = maker[n]
            follow[p.name].append((s.name, LATENCY + HOP * hops + size * hops / RATE))
    ranks = {}

    def rank(n):
        if n not in ranks:
            ranks[n] = by_name[n].cost + max([c + rank(f) for f, c in follow[n]], default=0.0)
        return ranks[n]

    done, there, free, gone = {}, {}, {"x": 0.0, "z": 0.0}, {}
    now, left, out = 0.0, list(steps), []
    while left:
        best, later = None, []
        for s in left:
            if any(p not in done for p in s.after) or any(n not in there for n in s.needs):
                continue
            at = max([done[p] for p in s.after] + [there[n] for n in s.needs] + [0.0])
            at = max([at] + [free[link] - WINDOW for _, link, _, _ in s.sends])
            if at > now + 1e-9:
                later.append(at)
            elif best is None or rank(s.name) > rank(best.name):
                best = s
        if best is None:
            now = min(later)
            continue
        left.remove(best)
        now += best.cost
        done[best.name] = now
        for n, link, size, hops in best.sends:
            free[link] = max(now, free[link]) + size * hops / RATE
            there[n] = free[link] + LATENCY + HOP * hops
            gone[n] = there[n] + 4.0
        past = [n for n in gone if gone[n] < now]
        for n in past:
            del gone[n]
        out.append((best, past))
    out.append((None, list(gone)))
    return out


def kernel(
    ids, live, a_hbm, c_hbm, vt_hbm, out,
    a0, a1, a2, c, vt, s, h, acc, stage,
    ax2, ax1, axm, az, azm, bz, bzm, bx,
    sems, occ_s, in_s,
):
    me, o = lax.axis_index("pair"), lax.axis_index("occ")
    n_occ = lax.axis_size("occ")
    z, x = me // NX, me % NX
    m = 1 - 2 * (o % 2)
    n_i = c.shape[2]
    rows_a, rows_b = pl.ds(0, CUT), pl.ds(CUT, ROWS - CUT)

    def zat(d):
        return (z + d * m + NZ) % NZ

    def xat(d):
        return (x + d * m + NX) % NX

    z_up, z_down = zat(1) * NX + x, zat(-1) * NX + x
    x_up, x_down, x_far = z * NX + xat(1), z * NX + xat(-1), z * NX + xat(2)

    parts = (a0, a1, a2)
    slots = NX * GROUP

    def load_a(g, k):
        return pltpu.make_async_copy(
            a_hbm.at[pl.ds(zat(far_first(k)) * slots, slots)],
            parts[g].at[pl.ds((k - FIRST[g][0]) * slots, slots)],
            in_s.at[k],
        )

    load_c = pltpu.make_async_copy(c_hbm, c.at[pl.ds(0, OWNERS * OWNED)], in_s.at[NZ])
    load_v = pltpu.make_async_copy(vt_hbm, vt, in_s.at[NZ + 1])
    load_c.start()
    for g, (lo, hi) in enumerate(FIRST):
        for k in range(lo, hi):
            load_a(g, k).start()
    load_v.start()

    barrier = pltpu.get_barrier_semaphore()
    for to in (z_up, z_down, x_up, x_down, x_far):
        pl.semaphore_signal(barrier, inc=1, device_id={"pair": to}, device_id_type=MESH)
    for d in range(1, n_occ):
        pl.semaphore_signal(
            barrier, inc=1, device_id={"occ": (o + d) % n_occ}, device_id_type=MESH
        )
    c[OWNERS * OWNED] = jnp.zeros((BS, n_i), c.dtype)
    load_c.wait()

    def transform(part, at, q):
        on = [live[0, q * GROUP + j] for j in range(GROUP)]
        seen, before = 0, []
        for j in range(GROUP):
            before.append(seen)
            seen = seen + on[j]
        blocks, picks = [], [[] for _ in range(OWNED)]
        for n in range(LIVE):
            slot = 0
            for j in range(1, GROUP):
                slot = slot + jnp.where(jnp.logical_and(on[j] != 0, before[j] == n), j, 0)
            mu, nu = ids[0, 0, q * GROUP + slot], ids[1, 0, q * GROUP + slot]
            blocks.append(part[at + slot])
            for b in range(OWNED):
                hit = jnp.logical_and(seen > n, nu == q * OWNED + b)
                picks[b].append(c[jnp.where(hit, mu, OWNERS * OWNED)])
        left = [t[:, :BS] for t in blocks]
        right = [t[:, BS:] for t in blocks]
        lhs = jnp.concatenate(
            [jnp.concatenate(left, axis=1), jnp.concatenate(right, axis=1)], axis=0
        )
        rhs = jnp.concatenate([jnp.concatenate(p, axis=0) for p in picks], axis=1)
        got = jnp.dot(lhs, rhs, preferred_element_type=jnp.float32).astype(s.dtype)
        for b in range(OWNED):
            for side in range(2):
                s[q // NX, q % NX, pl.ds(b * BS, BS), pl.ds(side * n_i, n_i)] = got[
                    side * BS : (side + 1) * BS, b * n_i : (b + 1) * n_i
                ]

    copies, numbers = {}, {}

    def message(name, to, src, dst):
        numbers[name] = len(numbers)

        def make():
            return pltpu.make_async_remote_copy(
                src_ref=src(), dst_ref=dst(),
                send_sem=sems.at[0, numbers[name]], recv_sem=sems.at[1, numbers[name]],
                device_id={"pair": to}, device_id_type=MESH,
            )

        copies[name] = make

    def stay(name, to, part):
        message(name, to, part, part)

    steps = []
    one_a, one_b = CUT * s.shape[3] * 2, (ROWS - CUT) * s.shape[3] * 2
    start_cost = 0.04

    def add_cost(size):
        return 0.05 + size / 4e5

    def step(name, after=(), needs=(), sends=(), run=lambda: None, cost=start_cost):
        steps.append(Step(name, cost, list(after), list(needs), list(sends), run))

    def add(at, *terms, into=s):
        def run():
            total = s[at].astype(jnp.float32)
            for t in terms:
                total += t().astype(jnp.float32)
            into[at] = total.astype(into.dtype)

        return run

    place = {far_first(k): k for k in range(NZ)}
    ready = {k: ("transform", g) for g, (lo, hi) in enumerate(FIRST) for k in range(lo, hi)}

    def run_transform(g):
        lo, hi = FIRST[g]

        def run():
            for k in range(lo, hi):
                load_a(g, k).wait()

            @pl.loop(0, (hi - lo) * NX)
            def _(n):
                q = zat(far_first(lo + n // NX)) * NX + n % NX
                transform(parts[g], n * GROUP, q)

            if g == 0:
                pl.semaphore_wait(barrier, 5 + n_occ - 1)

        return run

    for g, (lo, hi) in enumerate(FIRST):
        step(
            ready[lo], [("transform", g - 1)] if g else [], run=run_transform(g),
            cost=0.55 * (hi - lo) + (2.0 if g == 0 else 0.0),
        )

    for k in range(NZ):
        d = far_first(k)
        message(("ax2", k), x_up, lambda d=d: s.at[zat(d), xat(2), rows_a], lambda k=k: ax2.at[k])
        message(("ax1", k), x_up, lambda d=d: s.at[zat(d), xat(1), rows_a], lambda k=k: ax1.at[k])
        message(("axm", k), x_down, lambda d=d: s.at[zat(d), xat(-1), rows_a], lambda k=k: axm.at[k])
        step(("ax2", k), [ready[k]], [], [(("ax2", k), "x", one_a, 1)])
        step(("axm", k), [ready[k]], [], [(("axm", k), "x", one_a, 1)])
        step(
            ("ax1", k), [ready[k]], [("ax2", k)], [(("ax1", k), "x", one_a, 1)],
            add((zat(d), xat(1), rows_a), lambda k=k: ax2[k]), add_cost(one_a),
        )
        step(
            ("ax", k), [ready[k]], [("ax1", k), ("axm", k)], [],
            add((zat(d), x, rows_a), lambda k=k: ax1[k], lambda k=k: axm[k]), 1.3 * add_cost(one_a),
        )

    for f in range(HALVES):
        lanes = pl.ds(f * n_i, n_i)
        size = one_a // HALVES
        for kind, hops, to, buf, sign in (("az", UP, z_up, az, 1), ("azm", DOWN, z_down, azm, -1)):
            for t in range(hops):
                d = sign * (hops - t)
                message(
                    (kind, t, f), to,
                    lambda d=d, lanes=lanes: s.at[zat(d), x, rows_a, lanes],
                    lambda t=t, lanes=lanes, buf=buf: buf.at[t, :, lanes],
                )
                if t:
                    run = add((zat(d), x, rows_a, lanes), lambda t=t, lanes=lanes, buf=buf: buf[t - 1, :, lanes])
                else:
                    run = lambda: None
                step(
                    (kind, t, f), [("ax", place[d])], [(kind, t - 1, f)] if t else [],
                    [((kind, t, f), "z", size, 1)], run, add_cost(size) if t else start_cost,
                )
        step(
            ("own a", f), [("ax", place[0])], [("az", UP - 1, f), ("azm", DOWN - 1, f)], [],
            add(
                (z, x, rows_a, lanes),
                lambda lanes=lanes: az[UP - 1, :, lanes], lambda lanes=lanes: azm[DOWN - 1, :, lanes], into=h,
            ), 1.5 * add_cost(size),
        )

    for j, dx in enumerate((2, 1, -1, 0)):
        for kind, hops, to, buf, sign in (("bz", UP, z_up, bz, 1), ("bzm", DOWN, z_down, bzm, -1)):
            for t in range(hops):
                d = sign * (hops - t)
                message(
                    (kind, t, j), to,
                    lambda d=d, dx=dx: s.at[zat(d), xat(dx), rows_b],
                    lambda t=t, j=j, buf=buf: buf.at[t, j],
                )
                if t:
                    run = add((zat(d), xat(dx), rows_b), lambda t=t, j=j, buf=buf: buf[t - 1, j])
                else:
                    run = lambda: None
                step(
                    (kind, t, j), [ready[place[d]]], [(kind, t - 1, j)] if t else [],
                    [((kind, t, j), "z", one_b, 1)], run, add_cost(one_b) if t else start_cost,
                )
        if dx:
            to = {2: x_far, 1: x_up, -1: x_down}[dx]
            message(("bx", j), to, lambda dx=dx: s.at[z, xat(dx), rows_b], lambda j=j: bx.at[j])
        step(
            ("b", j), [ready[place[0]]], [("bz", UP - 1, j), ("bzm", DOWN - 1, j)],
            [(("bx", j), "x", one_b, abs(dx))] if dx else [],
            add((z, xat(dx), rows_b), lambda j=j: bz[UP - 1, j], lambda j=j: bzm[DOWN - 1, j]), 1.3 * add_cost(one_b),
        )

    for j, (to, dx) in enumerate(((x_far, 2), (x_up, 1), (x_down, 1))):
        stay(("gb", j), to, lambda: h.at[z, x, rows_b])
    step(
        ("own b",), [("b", 3)], [("bx", j) for j in range(3)],
        [(("gb", 0), "x", one_b, 2), (("gb", 1), "x", one_b, 1), (("gb", 2), "x", one_b, 1)],
        add((z, x, rows_b), lambda: bx[0], lambda: bx[1], lambda: bx[2], into=h), 2 * add_cost(one_b),
    )
    for j, dx in enumerate((2, -1, 1, 0)):
        for kind, hops, to, sign in (("gbz", UP, z_up, -1), ("gbzm", DOWN, z_down, 1)):
            for t in range(hops):
                stay((kind, t, j), to, lambda t=t, dx=dx, sign=sign: h.at[zat(sign * t), xat(dx), rows_b])
                needs = [(kind, t - 1, j)] if t else ([("gb", j)] if dx else [])
                step((kind, t, j), [] if t or dx else [("own b",)], needs, [((kind, t, j), "z", one_b, 1)])
    for f in range(HALVES):
        lanes = pl.ds(f * n_i, n_i)
        for kind, hops, to, sign in (("gaz", UP, z_up, -1), ("gazm", DOWN, z_down, 1)):
            for t in range(hops):
                stay(
                    (kind, t, f), to,
                    lambda t=t, sign=sign, lanes=lanes: h.at[zat(sign * t), x, rows_a, lanes],
                )
                step(
                    (kind, t, f), [] if t else [("own a", f)], [(kind, t - 1, f)] if t else [],
                    [((kind, t, f), "z", one_a // HALVES, 1)],
                )
    for k in reversed(range(NZ)):
        d = far_first(k) if k else -UP
        after = [("own a", f) for f in range(HALVES)] if d == 0 else []
        halves = range(HALVES) if d else []
        came = [("gaz", -d - 1, f) if d < 0 else ("gazm", d - 1, f) for f in halves]
        stay(("gax0", d), x_up, lambda d=d: h.at[zat(d), x, rows_a])
        stay(("gaxm", d), x_down, lambda d=d: h.at[zat(d), x, rows_a])
        stay(("gax1", d), x_up, lambda d=d: h.at[zat(d), xat(-1), rows_a])
        step(("gax0", d), after, came, [(("gax0", d), "x", one_a, 1)])
        step(("gaxm", d), after, came, [(("gaxm", d), "x", one_a, 1)])
        step(("gax1", d), [], [("gax0", d)], [(("gax1", d), "x", one_a, 1)])

    def multiply(d):
        def run():
            depth = NX * ROWS
            zz = zat(d)
            at = pl.ds(pl.multiple_of(zz * depth, 128), depth)
            acc[...] += jnp.dot(
                vt[:, at], h[zz].reshape(depth, h.shape[3]), preferred_element_type=jnp.float32
            )

        return run

    def clear():
        load_v.wait()
        acc[...] = jnp.zeros_like(acc)

    step(("clear",), [("own b",)], run=clear, cost=0.2)
    for k in reversed(range(NZ)):
        d = far_first(k) if k else -UP
        needs = [("gax0", d), ("gax1", d), ("gaxm", d)]
        if d == 0:
            needs += [("gb", j) for j in range(3)]
        else:
            needs += [("gbz", -d - 1, j) if d < 0 else ("gbzm", d - 1, j) for j in range(NX)]
        step(
            ("multiply", d), [("clear",)] + ([("own a", f) for f in range(HALVES)] if d == 0 else []), needs,
            run=multiply(d), cost=0.3,
        )

    waited, last = set(), []
    for st, past in in_order(steps):
        if st is None:
            last = past
            continue
        for n in st.needs:
            if n not in waited:
                waited.add(n)
                copies[n]().wait_recv()
        st.run()
        for n, _, _, _ in st.sends:
            copies[n]().start()
        for n in past:
            copies[n]().wait_send()

    turned = acc[...].T.astype(stage.dtype)
    part = stage.shape[2]
    for side in range(2):
        for d in range(n_occ):
            at = (side * n_occ + d) * part
            stage[d, side] = turned[at : at + part]

    def occ_copy(to, source, d):
        return pltpu.make_async_remote_copy(
            src_ref=stage.at[to], dst_ref=out.at[pl.ds(2 * source, 2)],
            send_sem=occ_s.at[0, d], recv_sem=occ_s.at[1, d],
            device_id={"occ": to}, device_id_type=MESH,
        )

    for d in range(1, n_occ):
        occ_copy((o + d) % n_occ, o, d).start()
    mine = pltpu.make_async_copy(stage.at[o], out.at[pl.ds(2 * o, 2)], occ_s.at[0, 0])
    mine.start()
    for n in last:
        copies[n]().wait_send()
    mine.wait()
    for d in range(1, n_occ):
        occ_copy((o + d) % n_occ, o, d).wait_send()
        src = (o + n_occ - d) % n_occ
        occ_copy(src, src, d).wait_recv()


N_MESSAGES = 3 * NZ + (UP + DOWN) * (HALVES + NX) + 3


def on_device(integrals, occ_coeffs, virt_coeffs, block_ids, live_mask):
    blocks = integrals[0]
    n_i = occ_coeffs.shape[1]
    n_a = virt_coeffs.shape[1]
    n_occ = lax.axis_size("occ")
    bf16, f32 = jnp.bfloat16, jnp.float32
    wide = 2 * n_i
    ra, rb = CUT, ROWS - CUT
    any_space, smem = pl.BlockSpec(memory_space=pl.ANY), pl.BlockSpec(memory_space=pltpu.SMEM)
    got = pl.pallas_call(
        kernel,
        out_shape=jax.ShapeDtypeStruct((2 * n_occ, n_i // n_occ, n_a), bf16),
        in_specs=[smem, smem, any_space, any_space, any_space],
        out_specs=pl.BlockSpec(memory_space=pltpu.VMEM),
        scratch_shapes=[
            *(pltpu.VMEM(((hi - lo) * NX * GROUP, *blocks.shape[1:]), bf16) for lo, hi in FIRST),
            pltpu.VMEM((OWNERS * OWNED + 1, BS, n_i), bf16),
            pltpu.VMEM((n_a, OWNERS * ROWS), bf16),
            pltpu.VMEM((NZ, NX, ROWS, wide), bf16),
            pltpu.VMEM((NZ, NX, ROWS, wide), bf16),
            pltpu.VMEM((n_a, wide), f32),
            pltpu.VMEM((n_occ, 2, n_i // n_occ, n_a), bf16),
            pltpu.VMEM((NZ, ra, wide), bf16),
            pltpu.VMEM((NZ, ra, wide), bf16),
            pltpu.VMEM((NZ, ra, wide), bf16),
            pltpu.VMEM((UP, ra, wide), bf16),
            pltpu.VMEM((DOWN, ra, wide), bf16),
            pltpu.VMEM((UP, NX, rb, wide), bf16),
            pltpu.VMEM((DOWN, NX, rb, wide), bf16),
            pltpu.VMEM((3, rb, wide), bf16),
            pltpu.SemaphoreType.DMA((2, 2 * N_MESSAGES)),
            pltpu.SemaphoreType.DMA((2, n_occ)),
            pltpu.SemaphoreType.DMA((NZ + 2,)),
        ],
        compiler_params=pltpu.CompilerParams(
            collective_id=0, has_side_effects=True, vmem_limit_bytes=63_400_000
        ),
    )(
        block_ids,
        live_mask,
        blocks,
        occ_coeffs.reshape(OWNERS * OWNED, BS, n_i),
        virt_coeffs.T,
    )
    return jnp.transpose(got, (1, 0, 2))


def solution(mesh):
    return jax.shard_map(
        on_device,
        mesh=mesh,
        in_specs=(
            P("pair", None, None, "occ"),
            P(),
            P(None, "pair"),
            P(None, "pair", None),
            P("pair", None),
        ),
        out_specs=P("occ", None, "pair"),
        check_vma=False,
    )
```

```python
import jax
import jax.numpy as jnp
from jax import lax
from jax.experimental import pallas as pl
from jax.experimental.pallas import tpu as pltpu
from jax.sharding import PartitionSpec as P

NZ, NX = 8, 4
OWNERS = NZ * NX
GROUP = 8
LIVE = 4
OWNED = 3
BS = 64
ROWS = OWNED * BS
CUT = 112
UP, DOWN = NZ // 2, NZ // 2 - 1
MESH = pl.DeviceIdType.MESH
FIRST = ((0, 2), (2, 5), (5, 8))
HALVES = 2
TOGETHER = 2

RATE, LATENCY, HOP, WINDOW = 80e3, 1.25, 0.65, 1.0


def far_first(k):
    return (NZ // 2 - (k + 1) // 2) * (1 - 2 * (k % 2))


class Step:
    def __init__(self, name, cost, after, needs, sends, run):
        self.name, self.cost, self.after, self.needs, self.sends, self.run = name, cost, after, needs, sends, run


def in_order(steps):
    by_name = {s.name: s for s in steps}
    maker = {m[0]: (s, m) for s in steps for m in s.sends}
    follow = {s.name: [] for s in steps}
    for s in steps:
        for p in s.after:
            follow[p].append((s.name, 0.0))
        for n in s.needs:
            p, (_, _, size, hops) = maker[n]
            follow[p.name].append((s.name, LATENCY + HOP * hops + size * hops / RATE))
    ranks = {}

    def rank(n):
        if n not in ranks:
            ranks[n] = by_name[n].cost + max([c + rank(f) for f, c in follow[n]], default=0.0)
        return ranks[n]

    done, there, free, gone = {}, {}, {"x": 0.0, "z": 0.0}, {}
    now, left, out = 0.0, list(steps), []
    while left:
        best, later = None, []
        for s in left:
            if any(p not in done for p in s.after) or any(n not in there for n in s.needs):
                continue
            at = max([done[p] for p in s.after] + [there[n] for n in s.needs] + [0.0])
            at = max([at] + [free[link] - WINDOW for _, link, _, _ in s.sends])
            if at > now + 1e-9:
                later.append(at)
            elif best is None or rank(s.name) > rank(best.name):
                best = s
        if best is None:
            now = min(later)
            continue
        left.remove(best)
        now += best.cost
        done[best.name] = now
        for n, link, size, hops in best.sends:
            free[link] = max(now, free[link]) + size * hops / RATE
            there[n] = free[link] + LATENCY + HOP * hops
            gone[n] = there[n] + 4.0
        past = [n for n in gone if gone[n] < now]
        for n in past:
            del gone[n]
        out.append((best, past))
    out.append((None, list(gone)))
    return out


def kernel(
    ids, live, a_hbm, c_hbm, vt_hbm, out,
    a0, a1, a2, c, vt, s, h, acc, stage,
    ax2, ax1, axm, az, azm, bz, bzm, bx,
    sems, occ_s, in_s,
):
    me, o = lax.axis_index("pair"), lax.axis_index("occ")
    n_occ = lax.axis_size("occ")
    z, x = me // NX, me % NX
    m = 1 - 2 * (o % 2)
    n_i = c.shape[2]
    rows_a, rows_b = pl.ds(0, CUT), pl.ds(CUT, ROWS - CUT)

    def zat(d):
        return (z + d * m + NZ) % NZ

    def xat(d):
        return (x + d * m + NX) % NX

    z_up, z_down = zat(1) * NX + x, zat(-1) * NX + x
    x_up, x_down, x_far = z * NX + xat(1), z * NX + xat(-1), z * NX + xat(2)

    parts = (a0, a1, a2)
    slots = NX * GROUP

    def load_a(g, k):
        return pltpu.make_async_copy(
            a_hbm.at[pl.ds(zat(far_first(k)) * slots, slots)],
            parts[g].at[pl.ds((k - FIRST[g][0]) * slots, slots)],
            in_s.at[k],
        )

    load_c = pltpu.make_async_copy(c_hbm, c.at[pl.ds(0, OWNERS * OWNED)], in_s.at[NZ])
    load_v = pltpu.make_async_copy(vt_hbm, vt, in_s.at[NZ + 1])
    load_c.start()
    for g, (lo, hi) in enumerate(FIRST):
        for k in range(lo, hi):
            load_a(g, k).start()
    load_v.start()

    barrier = pltpu.get_barrier_semaphore()
    for to in (z_up, z_down, x_up, x_down, x_far):
        pl.semaphore_signal(barrier, inc=1, device_id={"pair": to}, device_id_type=MESH)
    for d in range(1, n_occ):
        pl.semaphore_signal(
            barrier, inc=1, device_id={"occ": (o + d) % n_occ}, device_id_type=MESH
        )
    c[OWNERS * OWNED] = jnp.zeros((BS, n_i), c.dtype)
    load_c.wait()

    def transform(part, at, q):
        slots = [0] * LIVE
        on = [live[0, q * GROUP + j] != 0 for j in range(GROUP)]
        for j in reversed(range(GROUP)):
            slots = [jnp.where(on[j], new, old) for new, old in zip([j] + slots[:-1], slots)]
        count = sum(jnp.where(t, 1, 0) for t in on)
        blocks, picks = [], [[] for _ in range(OWNED)]
        for n, slot in enumerate(slots):
            mu, nu = ids[0, 0, q * GROUP + slot], ids[1, 0, q * GROUP + slot]
            nu = jnp.where(count > n, nu, -1)
            blocks.append(part[at + slot])
            for b in range(OWNED):
                picks[b].append(c[jnp.where(nu == q * OWNED + b, mu, OWNERS * OWNED)])
        left = [t[:, :BS] for t in blocks]
        right = [t[:, BS:] for t in blocks]
        lhs = jnp.concatenate(
            [jnp.concatenate(left, axis=1), jnp.concatenate(right, axis=1)], axis=0
        )
        rhs = jnp.concatenate([jnp.concatenate(p, axis=0) for p in picks], axis=1)
        return jnp.dot(lhs, rhs, preferred_element_type=jnp.float32).astype(s.dtype)

    def put(got, zz, xx):
        for b in range(OWNED):
            for side in range(2):
                s[zz, xx, pl.ds(b * BS, BS), pl.ds(side * n_i, n_i)] = got[
                    side * BS : (side + 1) * BS, b * n_i : (b + 1) * n_i
                ]

    copies, numbers = {}, {}

    def message(name, to, src, dst):
        numbers[name] = len(numbers)

        def make():
            return pltpu.make_async_remote_copy(
                src_ref=src(), dst_ref=dst(),
                send_sem=sems.at[0, numbers[name]], recv_sem=sems.at[1, numbers[name]],
                device_id={"pair": to}, device_id_type=MESH,
            )

        copies[name] = make

    def stay(name, to, part):
        message(name, to, part, part)

    steps = []
    one_a, one_b = CUT * s.shape[3] * 2, (ROWS - CUT) * s.shape[3] * 2
    start_cost = 0.04

    def add_cost(size):
        return 0.05 + size / 4e5

    def step(name, after=(), needs=(), sends=(), run=lambda: None, cost=start_cost):
        steps.append(Step(name, cost, list(after), list(needs), list(sends), run))

    def add(at, *terms, into=s):
        def run():
            total = s[at].astype(jnp.float32)
            for t in terms:
                total += t().astype(jnp.float32)
            into[at] = total.astype(into.dtype)

        return run

    place = {far_first(k): k for k in range(NZ)}
    ready = {k: ("transform", g) for g, (lo, hi) in enumerate(FIRST) for k in range(lo, hi)}

    def run_transform(g):
        lo, hi = FIRST[g]

        def run():
            for k in range(lo, hi):
                load_a(g, k).wait()

            @pl.loop(lo, hi)
            def _(k):
                zz = zat(far_first(k))
                for xx in range(0, NX, TOGETHER):
                    got = [
                        transform(parts[g], ((k - lo) * NX + xx + n) * GROUP, zz * NX + xx + n)
                        for n in range(TOGETHER)
                    ]
                    for n in range(TOGETHER):
                        put(got[n], zz, xx + n)

            if g == 0:
                pl.semaphore_wait(barrier, 5 + n_occ - 1)

        return run

    for g, (lo, hi) in enumerate(FIRST):
        step(
            ready[lo], [("transform", g - 1)] if g else [], run=run_transform(g),
            cost=0.55 * (hi - lo) + (2.0 if g == 0 else 0.0),
        )

    for k in range(NZ):
        d = far_first(k)
        message(("ax2", k), x_up, lambda d=d: s.at[zat(d), xat(2), rows_a], lambda k=k: ax2.at[k])
        message(("ax1", k), x_up, lambda d=d: s.at[zat(d), xat(1), rows_a], lambda k=k: ax1.at[k])
        message(("axm", k), x_down, lambda d=d: s.at[zat(d), xat(-1), rows_a], lambda k=k: axm.at[k])
        step(("ax2", k), [ready[k]], [], [(("ax2", k), "x", one_a, 1)])
        step(("axm", k), [ready[k]], [], [(("axm", k), "x", one_a, 1)])
        step(
            ("ax1", k), [ready[k]], [("ax2", k)], [(("ax1", k), "x", one_a, 1)],
            add((zat(d), xat(1), rows_a), lambda k=k: ax2[k]), add_cost(one_a),
        )
        step(
            ("ax", k), [ready[k]], [("ax1", k), ("axm", k)], [],
            add((zat(d), x, rows_a), lambda k=k: ax1[k], lambda k=k: axm[k]), 1.3 * add_cost(one_a),
        )

    for f in range(HALVES):
        lanes = pl.ds(f * n_i, n_i)
        size = one_a // HALVES
        for kind, hops, to, buf, sign in (("az", UP, z_up, az, 1), ("azm", DOWN, z_down, azm, -1)):
            for t in range(hops):
                d = sign * (hops - t)
                message(
                    (kind, t, f), to,
                    lambda d=d, lanes=lanes: s.at[zat(d), x, rows_a, lanes],
                    lambda t=t, lanes=lanes, buf=buf: buf.at[t, :, lanes],
                )
                if t:
                    run = add((zat(d), x, rows_a, lanes), lambda t=t, lanes=lanes, buf=buf: buf[t - 1, :, lanes])
                else:
                    run = lambda: None
                step(
                    (kind, t, f), [("ax", place[d])], [(kind, t - 1, f)] if t else [],
                    [((kind, t, f), "z", size, 1)], run, add_cost(size) if t else start_cost,
                )
        step(
            ("own a", f), [("ax", place[0])], [("az", UP - 1, f), ("azm", DOWN - 1, f)], [],
            add(
                (z, x, rows_a, lanes),
                lambda lanes=lanes: az[UP - 1, :, lanes], lambda lanes=lanes: azm[DOWN - 1, :, lanes], into=h,
            ), 1.5 * add_cost(size),
        )

    for j, dx in enumerate((2, 1, -1, 0)):
        for kind, hops, to, buf, sign in (("bz", UP, z_up, bz, 1), ("bzm", DOWN, z_down, bzm, -1)):
            for t in range(hops):
                d = sign * (hops - t)
                message(
                    (kind, t, j), to,
                    lambda d=d, dx=dx: s.at[zat(d), xat(dx), rows_b],
                    lambda t=t, j=j, buf=buf: buf.at[t, j],
                )
                if t:
                    run = add((zat(d), xat(dx), rows_b), lambda t=t, j=j, buf=buf: buf[t - 1, j])
                else:
                    run = lambda: None
                step(
                    (kind, t, j), [ready[place[d]]], [(kind, t - 1, j)] if t else [],
                    [((kind, t, j), "z", one_b, 1)], run, add_cost(one_b) if t else start_cost,
                )
        if dx:
            to = {2: x_far, 1: x_up, -1: x_down}[dx]
            message(("bx", j), to, lambda dx=dx: s.at[z, xat(dx), rows_b], lambda j=j: bx.at[j])
        step(
            ("b", j), [ready[place[0]]], [("bz", UP - 1, j), ("bzm", DOWN - 1, j)],
            [(("bx", j), "x", one_b, abs(dx))] if dx else [],
            add((z, xat(dx), rows_b), lambda j=j: bz[UP - 1, j], lambda j=j: bzm[DOWN - 1, j]), 1.3 * add_cost(one_b),
        )

    for j, (to, dx) in enumerate(((x_far, 2), (x_up, 1), (x_down, 1))):
        stay(("gb", j), to, lambda: h.at[z, x, rows_b])
    step(
        ("own b",), [("b", 3)], [("bx", j) for j in range(3)],
        [(("gb", 0), "x", one_b, 2), (("gb", 1), "x", one_b, 1), (("gb", 2), "x", one_b, 1)],
        add((z, x, rows_b), lambda: bx[0], lambda: bx[1], lambda: bx[2], into=h), 2 * add_cost(one_b),
    )
    for j, dx in enumerate((2, -1, 1, 0)):
        for kind, hops, to, sign in (("gbz", UP, z_up, -1), ("gbzm", DOWN, z_down, 1)):
            for t in range(hops):
                stay((kind, t, j), to, lambda t=t, dx=dx, sign=sign: h.at[zat(sign * t), xat(dx), rows_b])
                needs = [(kind, t - 1, j)] if t else ([("gb", j)] if dx else [])
                step((kind, t, j), [] if t or dx else [("own b",)], needs, [((kind, t, j), "z", one_b, 1)])
    for f in range(HALVES):
        lanes = pl.ds(f * n_i, n_i)
        for kind, hops, to, sign in (("gaz", UP, z_up, -1), ("gazm", DOWN, z_down, 1)):
            for t in range(hops):
                stay(
                    (kind, t, f), to,
                    lambda t=t, sign=sign, lanes=lanes: h.at[zat(sign * t), x, rows_a, lanes],
                )
                step(
                    (kind, t, f), [] if t else [("own a", f)], [(kind, t - 1, f)] if t else [],
                    [((kind, t, f), "z", one_a // HALVES, 1)],
                )
    for k in reversed(range(NZ)):
        d = far_first(k) if k else -UP
        after = [("own a", f) for f in range(HALVES)] if d == 0 else []
        halves = range(HALVES) if d else []
        came = [("gaz", -d - 1, f) if d < 0 else ("gazm", d - 1, f) for f in halves]
        stay(("gax0", d), x_up, lambda d=d: h.at[zat(d), x, rows_a])
        stay(("gaxm", d), x_down, lambda d=d: h.at[zat(d), x, rows_a])
        stay(("gax1", d), x_up, lambda d=d: h.at[zat(d), xat(-1), rows_a])
        step(("gax0", d), after, came, [(("gax0", d), "x", one_a, 1)])
        step(("gaxm", d), after, came, [(("gaxm", d), "x", one_a, 1)])
        step(("gax1", d), [], [("gax0", d)], [(("gax1", d), "x", one_a, 1)])

    def multiply(d):
        def run():
            depth = NX * ROWS
            zz = zat(d)
            at = pl.ds(pl.multiple_of(zz * depth, 128), depth)
            acc[...] += jnp.dot(
                vt[:, at], h[zz].reshape(depth, h.shape[3]), preferred_element_type=jnp.float32
            )

        return run

    def clear():
        load_v.wait()
        acc[...] = jnp.zeros_like(acc)

    step(("clear",), [("own b",)], run=clear, cost=0.2)
    for k in reversed(range(NZ)):
        d = far_first(k) if k else -UP
        needs = [("gax0", d), ("gax1", d), ("gaxm", d)]
        if d == 0:
            needs += [("gb", j) for j in range(3)]
        else:
            needs += [("gbz", -d - 1, j) if d < 0 else ("gbzm", d - 1, j) for j in range(NX)]
        step(
            ("multiply", d), [("clear",)] + ([("own a", f) for f in range(HALVES)] if d == 0 else []), needs,
            run=multiply(d), cost=0.3,
        )

    waited, last = set(), []
    for st, past in in_order(steps):
        if st is None:
            last = past
            continue
        for n in st.needs:
            if n not in waited:
                waited.add(n)
                copies[n]().wait_recv()
        st.run()
        for n, _, _, _ in st.sends:
            copies[n]().start()
        for n in past:
            copies[n]().wait_send()

    turned = acc[...].T.astype(stage.dtype)
    part = stage.shape[2]
    for side in range(2):
        for d in range(n_occ):
            at = (side * n_occ + d) * part
            stage[d, side] = turned[at : at + part]

    def occ_copy(to, source, d):
        return pltpu.make_async_remote_copy(
            src_ref=stage.at[to], dst_ref=out.at[pl.ds(2 * source, 2)],
            send_sem=occ_s.at[0, d], recv_sem=occ_s.at[1, d],
            device_id={"occ": to}, device_id_type=MESH,
        )

    for d in range(1, n_occ):
        occ_copy((o + d) % n_occ, o, d).start()
    mine = pltpu.make_async_copy(stage.at[o], out.at[pl.ds(2 * o, 2)], occ_s.at[0, 0])
    mine.start()
    for n in last:
        copies[n]().wait_send()
    mine.wait()
    for d in range(1, n_occ):
        occ_copy((o + d) % n_occ, o, d).wait_send()
        src = (o + n_occ - d) % n_occ
        occ_copy(src, src, d).wait_recv()


N_MESSAGES = 3 * NZ + (UP + DOWN) * (HALVES + NX) + 3


def on_device(integrals, occ_coeffs, virt_coeffs, block_ids, live_mask):
    blocks = integrals[0]
    n_i = occ_coeffs.shape[1]
    n_a = virt_coeffs.shape[1]
    n_occ = lax.axis_size("occ")
    bf16, f32 = jnp.bfloat16, jnp.float32
    wide = 2 * n_i
    ra, rb = CUT, ROWS - CUT
    any_space, smem = pl.BlockSpec(memory_space=pl.ANY), pl.BlockSpec(memory_space=pltpu.SMEM)
    got = pl.pallas_call(
        kernel,
        out_shape=jax.ShapeDtypeStruct((2 * n_occ, n_i // n_occ, n_a), bf16),
        in_specs=[smem, smem, any_space, any_space, any_space],
        out_specs=pl.BlockSpec(memory_space=pltpu.VMEM),
        scratch_shapes=[
            *(pltpu.VMEM(((hi - lo) * NX * GROUP, *blocks.shape[1:]), bf16) for lo, hi in FIRST),
            pltpu.VMEM((OWNERS * OWNED + 1, BS, n_i), bf16),
            pltpu.VMEM((n_a, OWNERS * ROWS), bf16),
            pltpu.VMEM((NZ, NX, ROWS, wide), bf16),
            pltpu.VMEM((NZ, NX, ROWS, wide), bf16),
            pltpu.VMEM((n_a, wide), f32),
            pltpu.VMEM((n_occ, 2, n_i // n_occ, n_a), bf16),
            pltpu.VMEM((NZ, ra, wide), bf16),
            pltpu.VMEM((NZ, ra, wide), bf16),
            pltpu.VMEM((NZ, ra, wide), bf16),
            pltpu.VMEM((UP, ra, wide), bf16),
            pltpu.VMEM((DOWN, ra, wide), bf16),
            pltpu.VMEM((UP, NX, rb, wide), bf16),
            pltpu.VMEM((DOWN, NX, rb, wide), bf16),
            pltpu.VMEM((3, rb, wide), bf16),
            pltpu.SemaphoreType.DMA((2, 2 * N_MESSAGES)),
            pltpu.SemaphoreType.DMA((2, n_occ)),
            pltpu.SemaphoreType.DMA((NZ + 2,)),
        ],
        compiler_params=pltpu.CompilerParams(
            collective_id=0, has_side_effects=True, vmem_limit_bytes=63_400_000
        ),
    )(
        block_ids,
        live_mask,
        blocks,
        occ_coeffs.reshape(OWNERS * OWNED, BS, n_i),
        virt_coeffs.T,
    )
    return jnp.transpose(got, (1, 0, 2))


def solution(mesh):
    return jax.shard_map(
        on_device,
        mesh=mesh,
        in_specs=(
            P("pair", None, None, "occ"),
            P(),
            P(None, "pair"),
            P(None, "pair", None),
            P("pair", None),
        ),
        out_specs=P("occ", None, "pair"),
        check_vma=False,
    )
```

```python
import jax
import jax.numpy as jnp
from jax import lax
from jax.experimental import pallas as pl
from jax.experimental.pallas import tpu as pltpu
from jax.sharding import PartitionSpec as P

NZ, NX = 8, 4
OWNERS = NZ * NX
GROUP = 8
LIVE = 4
OWNED = 3
BS = 64
ROWS = OWNED * BS
CUT = 112
UP, DOWN = NZ // 2, NZ // 2 - 1
MESH = pl.DeviceIdType.MESH
FIRST = ((0, 1), (1, 2), (2, 8))
HALVES = 2
TOGETHER = 2

RATE, LATENCY, HOP, WINDOW = 80000.0, 0.5, 0.65, 2.091
LEAN = {'ax': -6.5, 'ax1': 31.9, 'ax2': -1.2, 'axm': -2.3, 'az': 30.0, 'azm': 10.6, 'b': -38.2, 'bz': 0.5, 'bzm': 6.9, 'clear': 0.7, 'gax0': 4.7, 'gax1': 32.0, 'gaxm': -14.0, 'gaz': 9.3, 'gazm': 20.1, 'gbz': 9.1, 'gbzm': -29.4, 'multiply': 13.1, 'own a': -24.3, 'own b': -19.8, 'transform': -55.9}


def far_first(k):
    return (NZ // 2 - (k + 1) // 2) * (1 - 2 * (k % 2))


class Step:
    def __init__(self, name, cost, after, needs, sends, run):
        self.name, self.cost, self.after, self.needs, self.sends, self.run = name, cost, after, needs, sends, run


def in_order(steps):
    by_name = {s.name: s for s in steps}
    maker = {m[0]: (s, m) for s in steps for m in s.sends}
    follow = {s.name: [] for s in steps}
    for s in steps:
        for p in s.after:
            follow[p].append((s.name, 0.0))
        for n in s.needs:
            p, (_, _, size, hops) = maker[n]
            follow[p.name].append((s.name, LATENCY + HOP * hops + size * hops / RATE))
    ranks = {}

    def rank(n):
        if n not in ranks:
            ranks[n] = by_name[n].cost + max([c + rank(f) for f, c in follow[n]], default=0.0)
        return ranks[n]

    def lean(n):
        return rank(n) + LEAN.get(n[0], 0.0)

    done, there, free, gone = {}, {}, {"x": 0.0, "z": 0.0}, {}
    now, left, out = 0.0, list(steps), []
    while left:
        best, later = None, []
        for s in left:
            if any(p not in done for p in s.after) or any(n not in there for n in s.needs):
                continue
            at = max([done[p] for p in s.after] + [there[n] for n in s.needs] + [0.0])
            at = max([at] + [free[link] - WINDOW for _, link, _, _ in s.sends])
            if at > now + 1e-9:
                later.append(at)
            elif best is None or lean(s.name) > lean(best.name):
                best = s
        if best is None:
            now = min(later)
            continue
        left.remove(best)
        now += best.cost
        done[best.name] = now
        for n, link, size, hops in best.sends:
            free[link] = max(now, free[link]) + size * hops / RATE
            there[n] = free[link] + LATENCY + HOP * hops
            gone[n] = there[n] + 4.0
        past = [n for n in gone if gone[n] < now]
        for n in past:
            del gone[n]
        out.append((best, past))
    out.append((None, list(gone)))
    return out


def kernel(
    ids, live, a_hbm, c_hbm, vt_hbm, out,
    a0, a1, a2, c, vt, s, h, acc, stage,
    ax2, ax1, axm, az, azm, bz, bzm, bx,
    sems, occ_s, in_s,
):
    me, o = lax.axis_index("pair"), lax.axis_index("occ")
    n_occ = lax.axis_size("occ")
    z, x = me // NX, me % NX
    m = 1 - 2 * (o % 2)
    n_i = c.shape[2]
    rows_a, rows_b = pl.ds(0, CUT), pl.ds(CUT, ROWS - CUT)

    def zat(d):
        return (z + d * m + NZ) % NZ

    def xat(d):
        return (x + d * m + NX) % NX

    z_up, z_down = zat(1) * NX + x, zat(-1) * NX + x
    x_up, x_down, x_far = z * NX + xat(1), z * NX + xat(-1), z * NX + xat(2)

    parts = (a0, a1, a2)
    slots = NX * GROUP

    def load_a(g, k):
        return pltpu.make_async_copy(
            a_hbm.at[pl.ds(zat(far_first(k)) * slots, slots)],
            parts[g].at[pl.ds((k - FIRST[g][0]) * slots, slots)],
            in_s.at[k],
        )

    load_c = pltpu.make_async_copy(c_hbm, c.at[pl.ds(0, OWNERS * OWNED)], in_s.at[NZ])
    load_v = pltpu.make_async_copy(vt_hbm, vt, in_s.at[NZ + 1])
    load_c.start()
    for g, (lo, hi) in enumerate(FIRST):
        for k in range(lo, hi):
            load_a(g, k).start()
    load_v.start()

    barrier = pltpu.get_barrier_semaphore()
    for to in (z_up, z_down, x_up, x_down, x_far):
        pl.semaphore_signal(barrier, inc=1, device_id={"pair": to}, device_id_type=MESH)
    for d in range(1, n_occ):
        pl.semaphore_signal(
            barrier, inc=1, device_id={"occ": (o + d) % n_occ}, device_id_type=MESH
        )
    c[OWNERS * OWNED] = jnp.zeros((BS, n_i), c.dtype)
    load_c.wait()

    def transform(part, at, q):
        slots = [0] * LIVE
        on = [live[0, q * GROUP + j] != 0 for j in range(GROUP)]
        for j in reversed(range(GROUP)):
            slots = [jnp.where(on[j], new, old) for new, old in zip([j] + slots[:-1], slots)]
        count = sum(jnp.where(t, 1, 0) for t in on)
        blocks, picks = [], [[] for _ in range(OWNED)]
        for n, slot in enumerate(slots):
            mu, nu = ids[0, 0, q * GROUP + slot], ids[1, 0, q * GROUP + slot]
            nu = jnp.where(count > n, nu, -1)
            blocks.append(part[at + slot])
            for b in range(OWNED):
                picks[b].append(c[jnp.where(nu == q * OWNED + b, mu, OWNERS * OWNED)])
        left = [t[:, :BS] for t in blocks]
        right = [t[:, BS:] for t in blocks]
        lhs = jnp.concatenate(
            [jnp.concatenate(left, axis=1), jnp.concatenate(right, axis=1)], axis=0
        )
        rhs = jnp.concatenate([jnp.concatenate(p, axis=0) for p in picks], axis=1)
        return jnp.dot(lhs, rhs, preferred_element_type=jnp.float32).astype(s.dtype)

    def put(got, zz, xx):
        for b in range(OWNED):
            for side in range(2):
                s[zz, xx, pl.ds(b * BS, BS), pl.ds(side * n_i, n_i)] = got[
                    side * BS : (side + 1) * BS, b * n_i : (b + 1) * n_i
                ]

    copies, numbers = {}, {}

    def message(name, to, src, dst):
        numbers[name] = len(numbers)

        def make():
            return pltpu.make_async_remote_copy(
                src_ref=src(), dst_ref=dst(),
                send_sem=sems.at[0, numbers[name]], recv_sem=sems.at[1, numbers[name]],
                device_id={"pair": to}, device_id_type=MESH,
            )

        copies[name] = make

    def stay(name, to, part):
        message(name, to, part, part)

    steps = []
    one_a, one_b = CUT * s.shape[3] * 2, (ROWS - CUT) * s.shape[3] * 2
    start_cost = 0.04

    def add_cost(size):
        return 0.05 + size / 4e5

    def step(name, after=(), needs=(), sends=(), run=lambda: None, cost=start_cost):
        steps.append(Step(name, cost, list(after), list(needs), list(sends), run))

    def add(at, *terms, into=s):
        def run():
            total = s[at].astype(jnp.float32)
            for t in terms:
                total += t().astype(jnp.float32)
            into[at] = total.astype(into.dtype)

        return run

    place = {far_first(k): k for k in range(NZ)}
    ready = {k: ("transform", g) for g, (lo, hi) in enumerate(FIRST) for k in range(lo, hi)}

    def run_transform(g):
        lo, hi = FIRST[g]

        def run():
            for k in range(lo, hi):
                load_a(g, k).wait()

            @pl.loop(lo, hi)
            def _(k):
                zz = zat(far_first(k))
                for xx in range(0, NX, TOGETHER):
                    got = [
                        transform(parts[g], ((k - lo) * NX + xx + n) * GROUP, zz * NX + xx + n)
                        for n in range(TOGETHER)
                    ]
                    for n in range(TOGETHER):
                        put(got[n], zz, xx + n)

            if g == 0:
                pl.semaphore_wait(barrier, 5 + n_occ - 1)

        return run

    for g, (lo, hi) in enumerate(FIRST):
        step(
            ready[lo], [("transform", g - 1)] if g else [], run=run_transform(g),
            cost=0.35 * (hi - lo) + (1.8 if g == 0 else 0.0),
        )

    for k in range(NZ):
        d = far_first(k)
        message(("ax2", k), x_up, lambda d=d: s.at[zat(d), xat(2), rows_a], lambda k=k: ax2.at[k])
        message(("ax1", k), x_up, lambda d=d: s.at[zat(d), xat(1), rows_a], lambda k=k: ax1.at[k])
        message(("axm", k), x_down, lambda d=d: s.at[zat(d), xat(-1), rows_a], lambda k=k: axm.at[k])
        step(("ax2", k), [ready[k]], [], [(("ax2", k), "x", one_a, 1)])
        step(("axm", k), [ready[k]], [], [(("axm", k), "x", one_a, 1)])
        step(
            ("ax1", k), [ready[k]], [("ax2", k)], [(("ax1", k), "x", one_a, 1)],
            add((zat(d), xat(1), rows_a), lambda k=k: ax2[k]), add_cost(one_a),
        )
        step(
            ("ax", k), [ready[k]], [("ax1", k), ("axm", k)], [],
            add((zat(d), x, rows_a), lambda k=k: ax1[k], lambda k=k: axm[k]), 1.3 * add_cost(one_a),
        )

    for f in range(HALVES):
        lanes = pl.ds(f * n_i, n_i)
        size = one_a // HALVES
        for kind, hops, to, buf, sign in (("az", UP, z_up, az, 1), ("azm", DOWN, z_down, azm, -1)):
            for t in range(hops):
                d = sign * (hops - t)
                message(
                    (kind, t, f), to,
                    lambda d=d, lanes=lanes: s.at[zat(d), x, rows_a, lanes],
                    lambda t=t, lanes=lanes, buf=buf: buf.at[t, :, lanes],
                )
                if t:
                    run = add((zat(d), x, rows_a, lanes), lambda t=t, lanes=lanes, buf=buf: buf[t - 1, :, lanes])
                else:
                    run = lambda: None
                step(
                    (kind, t, f), [("ax", place[d])], [(kind, t - 1, f)] if t else [],
                    [((kind, t, f), "z", size, 1)], run, add_cost(size) if t else start_cost,
                )
        step(
            ("own a", f), [("ax", place[0])], [("az", UP - 1, f), ("azm", DOWN - 1, f)], [],
            add(
                (z, x, rows_a, lanes),
                lambda lanes=lanes: az[UP - 1, :, lanes], lambda lanes=lanes: azm[DOWN - 1, :, lanes], into=h,
            ), 1.5 * add_cost(size),
        )

    for j, dx in enumerate((2, 1, -1, 0)):
        for kind, hops, to, buf, sign in (("bz", UP, z_up, bz, 1), ("bzm", DOWN, z_down, bzm, -1)):
            for t in range(hops):
                d = sign * (hops - t)
                message(
                    (kind, t, j), to,
                    lambda d=d, dx=dx: s.at[zat(d), xat(dx), rows_b],
                    lambda t=t, j=j, buf=buf: buf.at[t, j],
                )
                if t:
                    run = add((zat(d), xat(dx), rows_b), lambda t=t, j=j, buf=buf: buf[t - 1, j])
                else:
                    run = lambda: None
                step(
                    (kind, t, j), [ready[place[d]]], [(kind, t - 1, j)] if t else [],
                    [((kind, t, j), "z", one_b, 1)], run, add_cost(one_b) if t else start_cost,
                )
        if dx:
            to = {2: x_far, 1: x_up, -1: x_down}[dx]
            message(("bx", j), to, lambda dx=dx: s.at[z, xat(dx), rows_b], lambda j=j: bx.at[j])
        step(
            ("b", j), [ready[place[0]]], [("bz", UP - 1, j), ("bzm", DOWN - 1, j)],
            [(("bx", j), "x", one_b, abs(dx))] if dx else [],
            add((z, xat(dx), rows_b), lambda j=j: bz[UP - 1, j], lambda j=j: bzm[DOWN - 1, j]), 1.3 * add_cost(one_b),
        )

    for j, (to, dx) in enumerate(((x_far, 2), (x_up, 1), (x_down, 1))):
        stay(("gb", j), to, lambda: h.at[z, x, rows_b])
    step(
        ("own b",), [("b", 3)], [("bx", j) for j in range(3)],
        [(("gb", 0), "x", one_b, 2), (("gb", 1), "x", one_b, 1), (("gb", 2), "x", one_b, 1)],
        add((z, x, rows_b), lambda: bx[0], lambda: bx[1], lambda: bx[2], into=h), 2 * add_cost(one_b),
    )
    for j, dx in enumerate((2, -1, 1, 0)):
        for kind, hops, to, sign in (("gbz", UP, z_up, -1), ("gbzm", DOWN, z_down, 1)):
            for t in range(hops):
                stay((kind, t, j), to, lambda t=t, dx=dx, sign=sign: h.at[zat(sign * t), xat(dx), rows_b])
                needs = [(kind, t - 1, j)] if t else ([("gb", j)] if dx else [])
                step((kind, t, j), [] if t or dx else [("own b",)], needs, [((kind, t, j), "z", one_b, 1)])
    for f in range(HALVES):
        lanes = pl.ds(f * n_i, n_i)
        for kind, hops, to, sign in (("gaz", UP, z_up, -1), ("gazm", DOWN, z_down, 1)):
            for t in range(hops):
                stay(
                    (kind, t, f), to,
                    lambda t=t, sign=sign, lanes=lanes: h.at[zat(sign * t), x, rows_a, lanes],
                )
                step(
                    (kind, t, f), [] if t else [("own a", f)], [(kind, t - 1, f)] if t else [],
                    [((kind, t, f), "z", one_a // HALVES, 1)],
                )
    for k in reversed(range(NZ)):
        d = far_first(k) if k else -UP
        after = [("own a", f) for f in range(HALVES)] if d == 0 else []
        halves = range(HALVES) if d else []
        came = [("gaz", -d - 1, f) if d < 0 else ("gazm", d - 1, f) for f in halves]
        stay(("gax0", d), x_up, lambda d=d: h.at[zat(d), x, rows_a])
        stay(("gaxm", d), x_down, lambda d=d: h.at[zat(d), x, rows_a])
        stay(("gax1", d), x_up, lambda d=d: h.at[zat(d), xat(-1), rows_a])
        step(("gax0", d), after, came, [(("gax0", d), "x", one_a, 1)])
        step(("gaxm", d), after, came, [(("gaxm", d), "x", one_a, 1)])
        step(("gax1", d), [], [("gax0", d)], [(("gax1", d), "x", one_a, 1)])

    def multiply(d):
        def run():
            depth = NX * ROWS
            zz = zat(d)
            at = pl.ds(pl.multiple_of(zz * depth, 128), depth)
            acc[...] += jnp.dot(
                vt[:, at], h[zz].reshape(depth, h.shape[3]), preferred_element_type=jnp.float32
            )

        return run

    def clear():
        load_v.wait()
        acc[...] = jnp.zeros_like(acc)

    step(("clear",), [("own b",)], run=clear, cost=0.2)
    for k in reversed(range(NZ)):
        d = far_first(k) if k else -UP
        needs = [("gax0", d), ("gax1", d), ("gaxm", d)]
        if d == 0:
            needs += [("gb", j) for j in range(3)]
        else:
            needs += [("gbz", -d - 1, j) if d < 0 else ("gbzm", d - 1, j) for j in range(NX)]
        step(
            ("multiply", d), [("clear",)] + ([("own a", f) for f in range(HALVES)] if d == 0 else []), needs,
            run=multiply(d), cost=0.3,
        )

    waited, last = set(), []
    for st, past in in_order(steps):
        if st is None:
            last = past
            continue
        for n in st.needs:
            if n not in waited:
                waited.add(n)
                copies[n]().wait_recv()
        st.run()
        for n, _, _, _ in st.sends:
            copies[n]().start()
        for n in past:
            copies[n]().wait_send()

    turned = acc[...].T.astype(stage.dtype)
    part = stage.shape[2]
    for side in range(2):
        for d in range(n_occ):
            at = (side * n_occ + d) * part
            stage[d, side] = turned[at : at + part]

    def occ_copy(to, source, d):
        return pltpu.make_async_remote_copy(
            src_ref=stage.at[to], dst_ref=out.at[pl.ds(2 * source, 2)],
            send_sem=occ_s.at[0, d], recv_sem=occ_s.at[1, d],
            device_id={"occ": to}, device_id_type=MESH,
        )

    for d in range(1, n_occ):
        occ_copy((o + d) % n_occ, o, d).start()
    mine = pltpu.make_async_copy(stage.at[o], out.at[pl.ds(2 * o, 2)], occ_s.at[0, 0])
    mine.start()
    for n in last:
        copies[n]().wait_send()
    mine.wait()
    for d in range(1, n_occ):
        occ_copy((o + d) % n_occ, o, d).wait_send()
        src = (o + n_occ - d) % n_occ
        occ_copy(src, src, d).wait_recv()


N_MESSAGES = 3 * NZ + (UP + DOWN) * (HALVES + NX) + 3


def on_device(integrals, occ_coeffs, virt_coeffs, block_ids, live_mask):
    blocks = integrals[0]
    n_i = occ_coeffs.shape[1]
    n_a = virt_coeffs.shape[1]
    n_occ = lax.axis_size("occ")
    bf16, f32 = jnp.bfloat16, jnp.float32
    wide = 2 * n_i
    ra, rb = CUT, ROWS - CUT
    any_space, smem = pl.BlockSpec(memory_space=pl.ANY), pl.BlockSpec(memory_space=pltpu.SMEM)
    got = pl.pallas_call(
        kernel,
        out_shape=pltpu.VMEM((2 * n_occ, n_i // n_occ, n_a), bf16),
        in_specs=[smem, smem, any_space, any_space, any_space],
        out_specs=pl.BlockSpec(memory_space=pltpu.VMEM),
        scratch_shapes=[
            *(pltpu.VMEM(((hi - lo) * NX * GROUP, *blocks.shape[1:]), bf16) for lo, hi in FIRST),
            pltpu.VMEM((OWNERS * OWNED + 1, BS, n_i), bf16),
            pltpu.VMEM((n_a, OWNERS * ROWS), bf16),
            pltpu.VMEM((NZ, NX, ROWS, wide), bf16),
            pltpu.VMEM((NZ, NX, ROWS, wide), bf16),
            pltpu.VMEM((n_a, wide), f32),
            pltpu.VMEM((n_occ, 2, n_i // n_occ, n_a), bf16),
            pltpu.VMEM((NZ, ra, wide), bf16),
            pltpu.VMEM((NZ, ra, wide), bf16),
            pltpu.VMEM((NZ, ra, wide), bf16),
            pltpu.VMEM((UP, ra, wide), bf16),
            pltpu.VMEM((DOWN, ra, wide), bf16),
            pltpu.VMEM((UP, NX, rb, wide), bf16),
            pltpu.VMEM((DOWN, NX, rb, wide), bf16),
            pltpu.VMEM((3, rb, wide), bf16),
            pltpu.SemaphoreType.DMA((2, 2 * N_MESSAGES)),
            pltpu.SemaphoreType.DMA((2, n_occ)),
            pltpu.SemaphoreType.DMA((NZ + 2,)),
        ],
        compiler_params=pltpu.CompilerParams(
            collective_id=0, has_side_effects=True, vmem_limit_bytes=63_200_000
        ),
    )(
        block_ids,
        live_mask,
        blocks,
        occ_coeffs.reshape(OWNERS * OWNED, BS, n_i),
        virt_coeffs.T,
    )
    return jnp.transpose(got, (1, 0, 2))


def solution(mesh):
    return jax.shard_map(
        on_device,
        mesh=mesh,
        in_specs=(
            P("pair", None, None, "occ"),
            P(),
            P(None, "pair"),
            P(None, "pair", None),
            P("pair", None),
        ),
        out_specs=P("occ", None, "pair"),
        check_vma=False,
    )
```

```python
import jax
import jax.numpy as jnp
from jax import lax
from jax.experimental import pallas as pl
from jax.experimental.pallas import tpu as pltpu
from jax.sharding import PartitionSpec as P

NZ, NX = 8, 4
OWNERS = NZ * NX
GROUP = 8
LIVE = 4
OWNED = 3
BS = 64
ROWS = OWNED * BS
CUT = 112
UP, DOWN = NZ // 2, NZ // 2 - 1
MESH = pl.DeviceIdType.MESH
FIRST = ((0, 2), (2, 5), (5, 8))
HALVES = 2
TOGETHER = 2

RATE, LATENCY, HOP, WINDOW = 80000.0, 1.416, 0.65, 1.455
LEAN = {'ax': 15.1, 'ax1': 14.0, 'ax2': 3.5, 'axm': 5.6, 'az': -13.3, 'azm': -0.4, 'b': 40.3, 'bz': -14.2, 'bzm': -14.3, 'clear': -4.3, 'gax0': -11.3, 'gax1': 57.5, 'gaxm': -23.6, 'gaz': 118.3, 'gazm': -12.0, 'gbz': 27.5, 'gbzm': -25.4, 'multiply': -23.5, 'own a': -38.5, 'own b': 27.6, 'transform': -45.5}


def far_first(k):
    return (NZ // 2 - (k + 1) // 2) * (1 - 2 * (k % 2))


class Step:
    def __init__(self, name, cost, after, needs, sends, run):
        self.name, self.cost, self.after, self.needs, self.sends, self.run = name, cost, after, needs, sends, run


def in_order(steps):
    by_name = {s.name: s for s in steps}
    maker = {m[0]: (s, m) for s in steps for m in s.sends}
    follow = {s.name: [] for s in steps}
    for s in steps:
        for p in s.after:
            follow[p].append((s.name, 0.0))
        for n in s.needs:
            p, (_, _, size, hops) = maker[n]
            follow[p.name].append((s.name, LATENCY + HOP * hops + size * hops / RATE))
    ranks = {}

    def rank(n):
        if n not in ranks:
            ranks[n] = by_name[n].cost + max([c + rank(f) for f, c in follow[n]], default=0.0)
        return ranks[n]

    def lean(n):
        return rank(n) + LEAN.get(n[0], 0.0)

    done, there, free, gone = {}, {}, {"x": 0.0, "z": 0.0}, {}
    now, left, out = 0.0, list(steps), []
    while left:
        best, later = None, []
        for s in left:
            if any(p not in done for p in s.after) or any(n not in there for n in s.needs):
                continue
            at = max([done[p] for p in s.after] + [there[n] for n in s.needs] + [0.0])
            at = max([at] + [free[link] - WINDOW for _, link, _, _ in s.sends])
            if at > now + 1e-9:
                later.append(at)
            elif best is None or lean(s.name) > lean(best.name):
                best = s
        if best is None:
            now = min(later)
            continue
        left.remove(best)
        now += best.cost
        done[best.name] = now
        for n, link, size, hops in best.sends:
            free[link] = max(now, free[link]) + size * hops / RATE
            there[n] = free[link] + LATENCY + HOP * hops
            gone[n] = there[n] + 4.0
        past = [n for n in gone if gone[n] < now]
        for n in past:
            del gone[n]
        out.append((best, past))
    out.append((None, list(gone)))
    return out


def kernel(
    ids, live, a_hbm, c_hbm, vt_hbm, out,
    a0, a1, a2, c, vt, s, h, acc, stage,
    ax2, ax1, axm, az, azm, bz, bzm, bx,
    sems, occ_s, in_s,
):
    me, o = lax.axis_index("pair"), lax.axis_index("occ")
    n_occ = lax.axis_size("occ")
    z, x = me // NX, me % NX
    m = 1 - 2 * (o % 2)
    n_i = c.shape[2]
    rows_a, rows_b = pl.ds(0, CUT), pl.ds(CUT, ROWS - CUT)

    def zat(d):
        return (z + d * m + NZ) % NZ

    def xat(d):
        return (x + d * m + NX) % NX

    z_up, z_down = zat(1) * NX + x, zat(-1) * NX + x
    x_up, x_down, x_far = z * NX + xat(1), z * NX + xat(-1), z * NX + xat(2)

    parts = (a0, a1, a2)
    slots = NX * GROUP

    def load_a(g, k):
        return pltpu.make_async_copy(
            a_hbm.at[pl.ds(zat(far_first(k)) * slots, slots)],
            parts[g].at[pl.ds((k - FIRST[g][0]) * slots, slots)],
            in_s.at[k],
        )

    load_c = pltpu.make_async_copy(c_hbm, c.at[pl.ds(0, OWNERS * OWNED)], in_s.at[NZ])
    load_v = pltpu.make_async_copy(vt_hbm, vt, in_s.at[NZ + 1])
    load_c.start()
    for g, (lo, hi) in enumerate(FIRST):
        for k in range(lo, hi):
            load_a(g, k).start()
    load_v.start()

    barrier = pltpu.get_barrier_semaphore()
    for to in (z_up, z_down, x_up, x_down, x_far):
        pl.semaphore_signal(barrier, inc=1, device_id={"pair": to}, device_id_type=MESH)
    for d in range(1, n_occ):
        pl.semaphore_signal(
            barrier, inc=1, device_id={"occ": (o + d) % n_occ}, device_id_type=MESH
        )
    c[OWNERS * OWNED] = jnp.zeros((BS, n_i), c.dtype)
    load_c.wait()

    def transform(part, at, q):
        slots = [0] * LIVE
        on = [live[0, q * GROUP + j] != 0 for j in range(GROUP)]
        for j in reversed(range(GROUP)):
            slots = [jnp.where(on[j], new, old) for new, old in zip([j] + slots[:-1], slots)]
        count = sum(jnp.where(t, 1, 0) for t in on)
        blocks, picks = [], [[] for _ in range(OWNED)]
        for n, slot in enumerate(slots):
            mu, nu = ids[0, 0, q * GROUP + slot], ids[1, 0, q * GROUP + slot]
            nu = jnp.where(count > n, nu, -1)
            blocks.append(part[at + slot])
            for b in range(OWNED):
                picks[b].append(c[jnp.where(nu == q * OWNED + b, mu, OWNERS * OWNED)])
        left = [t[:, :BS] for t in blocks]
        right = [t[:, BS:] for t in blocks]
        lhs = jnp.concatenate(
            [jnp.concatenate(left, axis=1), jnp.concatenate(right, axis=1)], axis=0
        )
        rhs = jnp.concatenate([jnp.concatenate(p, axis=0) for p in picks], axis=1)
        return jnp.dot(lhs, rhs, preferred_element_type=jnp.float32).astype(s.dtype)

    def put(got, zz, xx):
        for b in range(OWNED):
            for side in range(2):
                s[zz, xx, pl.ds(b * BS, BS), pl.ds(side * n_i, n_i)] = got[
                    side * BS : (side + 1) * BS, b * n_i : (b + 1) * n_i
                ]

    copies, numbers = {}, {}

    def message(name, to, src, dst):
        numbers[name] = len(numbers)

        def make():
            return pltpu.make_async_remote_copy(
                src_ref=src(), dst_ref=dst(),
                send_sem=sems.at[0, numbers[name]], recv_sem=sems.at[1, numbers[name]],
                device_id={"pair": to}, device_id_type=MESH,
            )

        copies[name] = make

    def stay(name, to, part):
        message(name, to, part, part)

    steps = []
    one_a, one_b = CUT * s.shape[3] * 2, (ROWS - CUT) * s.shape[3] * 2
    start_cost = 0.04

    def add_cost(size):
        return 0.05 + size / 4e5

    def step(name, after=(), needs=(), sends=(), run=lambda: None, cost=start_cost):
        cost += 0.02 * (1 + len(needs) + len(sends))
        steps.append(Step(name, cost, list(after), list(needs), list(sends), run))

    def add(at, *terms, into=s):
        def run():
            total = s[at].astype(jnp.float32)
            for t in terms:
                total += t().astype(jnp.float32)
            into[at] = total.astype(into.dtype)

        return run

    place = {far_first(k): k for k in range(NZ)}
    ready = {k: ("transform", g) for g, (lo, hi) in enumerate(FIRST) for k in range(lo, hi)}

    def run_transform(g):
        lo, hi = FIRST[g]

        def run():
            for k in range(lo, hi):
                load_a(g, k).wait()

            @pl.loop(lo, hi)
            def _(k):
                zz = zat(far_first(k))
                for xx in range(0, NX, TOGETHER):
                    got = [
                        transform(parts[g], ((k - lo) * NX + xx + n) * GROUP, zz * NX + xx + n)
                        for n in range(TOGETHER)
                    ]
                    for n in range(TOGETHER):
                        put(got[n], zz, xx + n)

            if g == 0:
                pl.semaphore_wait(barrier, 5 + n_occ - 1)

        return run

    for g, (lo, hi) in enumerate(FIRST):
        step(
            ready[lo], [("transform", g - 1)] if g else [], run=run_transform(g),
            cost=0.35 * (hi - lo) + (1.8 if g == 0 else 0.0),
        )

    for k in range(NZ):
        d = far_first(k)
        message(("ax2", k), x_up, lambda d=d: s.at[zat(d), xat(2), rows_a], lambda k=k: ax2.at[k])
        message(("ax1", k), x_up, lambda d=d: s.at[zat(d), xat(1), rows_a], lambda k=k: ax1.at[k])
        message(("axm", k), x_down, lambda d=d: s.at[zat(d), xat(-1), rows_a], lambda k=k: axm.at[k])
        step(("ax2", k), [ready[k]], [], [(("ax2", k), "x", one_a, 1)])
        step(("axm", k), [ready[k]], [], [(("axm", k), "x", one_a, 1)])
        step(
            ("ax1", k), [ready[k]], [("ax2", k)], [(("ax1", k), "x", one_a, 1)],
            add((zat(d), xat(1), rows_a), lambda k=k: ax2[k]), add_cost(one_a),
        )
        step(
            ("ax", k), [ready[k]], [("ax1", k), ("axm", k)], [],
            add((zat(d), x, rows_a), lambda k=k: ax1[k], lambda k=k: axm[k]), 1.3 * add_cost(one_a),
        )

    for f in range(HALVES):
        lanes = pl.ds(f * n_i, n_i)
        size = one_a // HALVES
        for kind, hops, to, buf, sign in (("az", UP, z_up, az, 1), ("azm", DOWN, z_down, azm, -1)):
            for t in range(hops):
                d = sign * (hops - t)
                message(
                    (kind, t, f), to,
                    lambda d=d, lanes=lanes: s.at[zat(d), x, rows_a, lanes],
                    lambda t=t, lanes=lanes, buf=buf: buf.at[t, :, lanes],
                )
                if t:
                    run = add((zat(d), x, rows_a, lanes), lambda t=t, lanes=lanes, buf=buf: buf[t - 1, :, lanes])
                else:
                    run = lambda: None
                step(
                    (kind, t, f), [("ax", place[d])], [(kind, t - 1, f)] if t else [],
                    [((kind, t, f), "z", size, 1)], run, add_cost(size) if t else start_cost,
                )
        step(
            ("own a", f), [("ax", place[0])], [("az", UP - 1, f), ("azm", DOWN - 1, f)], [],
            add(
                (z, x, rows_a, lanes),
                lambda lanes=lanes: az[UP - 1, :, lanes], lambda lanes=lanes: azm[DOWN - 1, :, lanes], into=h,
            ), 1.5 * add_cost(size),
        )

    for j, dx in enumerate((2, 1, -1, 0)):
        for kind, hops, to, buf, sign in (("bz", UP, z_up, bz, 1), ("bzm", DOWN, z_down, bzm, -1)):
            for t in range(hops):
                d = sign * (hops - t)
                message(
                    (kind, t, j), to,
                    lambda d=d, dx=dx: s.at[zat(d), xat(dx), rows_b],
                    lambda t=t, j=j, buf=buf: buf.at[t, j],
                )
                if t:
                    run = add((zat(d), xat(dx), rows_b), lambda t=t, j=j, buf=buf: buf[t - 1, j])
                else:
                    run = lambda: None
                step(
                    (kind, t, j), [ready[place[d]]], [(kind, t - 1, j)] if t else [],
                    [((kind, t, j), "z", one_b, 1)], run, add_cost(one_b) if t else start_cost,
                )
        if dx:
            to = {2: x_far, 1: x_up, -1: x_down}[dx]
            message(("bx", j), to, lambda dx=dx: s.at[z, xat(dx), rows_b], lambda j=j: bx.at[j])
        step(
            ("b", j), [ready[place[0]]], [("bz", UP - 1, j), ("bzm", DOWN - 1, j)],
            [(("bx", j), "x", one_b, abs(dx))] if dx else [],
            add((z, xat(dx), rows_b), lambda j=j: bz[UP - 1, j], lambda j=j: bzm[DOWN - 1, j]), 1.3 * add_cost(one_b),
        )

    for j, (to, dx) in enumerate(((x_far, 2), (x_up, 1), (x_down, 1))):
        stay(("gb", j), to, lambda: h.at[z, x, rows_b])
    step(
        ("own b",), [("b", 3)], [("bx", j) for j in range(3)],
        [(("gb", 0), "x", one_b, 2), (("gb", 1), "x", one_b, 1), (("gb", 2), "x", one_b, 1)],
        add((z, x, rows_b), lambda: bx[0], lambda: bx[1], lambda: bx[2], into=h), 2 * add_cost(one_b),
    )
    for j, dx in enumerate((2, -1, 1, 0)):
        for kind, hops, to, sign in (("gbz", UP, z_up, -1), ("gbzm", DOWN, z_down, 1)):
            for t in range(hops):
                stay((kind, t, j), to, lambda t=t, dx=dx, sign=sign: h.at[zat(sign * t), xat(dx), rows_b])
                needs = [(kind, t - 1, j)] if t else ([("gb", j)] if dx else [])
                step((kind, t, j), [] if t or dx else [("own b",)], needs, [((kind, t, j), "z", one_b, 1)])
    for f in range(HALVES):
        lanes = pl.ds(f * n_i, n_i)
        for kind, hops, to, sign in (("gaz", UP, z_up, -1), ("gazm", DOWN, z_down, 1)):
            for t in range(hops):
                stay(
                    (kind, t, f), to,
                    lambda t=t, sign=sign, lanes=lanes: h.at[zat(sign * t), x, rows_a, lanes],
                )
                step(
                    (kind, t, f), [] if t else [("own a", f)], [(kind, t - 1, f)] if t else [],
                    [((kind, t, f), "z", one_a // HALVES, 1)],
                )
    for k in reversed(range(NZ)):
        d = far_first(k) if k else -UP
        after = [("own a", f) for f in range(HALVES)] if d == 0 else []
        halves = range(HALVES) if d else []
        came = [("gaz", -d - 1, f) if d < 0 else ("gazm", d - 1, f) for f in halves]
        stay(("gax0", d), x_up, lambda d=d: h.at[zat(d), x, rows_a])
        stay(("gaxm", d), x_down, lambda d=d: h.at[zat(d), x, rows_a])
        stay(("gax1", d), x_up, lambda d=d: h.at[zat(d), xat(-1), rows_a])
        step(("gax0", d), after, came, [(("gax0", d), "x", one_a, 1)])
        step(("gaxm", d), after, came, [(("gaxm", d), "x", one_a, 1)])
        step(("gax1", d), [], [("gax0", d)], [(("gax1", d), "x", one_a, 1)])

    def multiply(d):
        def run():
            depth = NX * ROWS
            zz = zat(d)
            at = pl.ds(pl.multiple_of(zz * depth, 128), depth)
            acc[...] += jnp.dot(
                vt[:, at], h[zz].reshape(depth, h.shape[3]), preferred_element_type=jnp.float32
            )

        return run

    def clear():
        load_v.wait()
        acc[...] = jnp.zeros_like(acc)

    step(("clear",), [("own b",)], run=clear, cost=0.2)
    for k in reversed(range(NZ)):
        d = far_first(k) if k else -UP
        needs = [("gax0", d), ("gax1", d), ("gaxm", d)]
        if d == 0:
            needs += [("gb", j) for j in range(3)]
        else:
            needs += [("gbz", -d - 1, j) if d < 0 else ("gbzm", d - 1, j) for j in range(NX)]
        step(
            ("multiply", d), [("clear",)] + ([("own a", f) for f in range(HALVES)] if d == 0 else []), needs,
            run=multiply(d), cost=0.3,
        )

    waited, last = set(), []
    for st, past in in_order(steps):
        if st is None:
            last = past
            continue
        for n in st.needs:
            if n not in waited:
                waited.add(n)
                copies[n]().wait_recv()
        st.run()
        for n, _, _, _ in st.sends:
            copies[n]().start()
        for n in past:
            copies[n]().wait_send()

    turned = acc[...].T.astype(stage.dtype)
    part = stage.shape[2]
    for side in range(2):
        for d in range(n_occ):
            at = (side * n_occ + d) * part
            stage[d, side] = turned[at : at + part]

    def occ_copy(to, source, d):
        return pltpu.make_async_remote_copy(
            src_ref=stage.at[to], dst_ref=out.at[pl.ds(2 * source, 2)],
            send_sem=occ_s.at[0, d], recv_sem=occ_s.at[1, d],
            device_id={"occ": to}, device_id_type=MESH,
        )

    for d in range(1, n_occ):
        occ_copy((o + d) % n_occ, o, d).start()
    mine = pltpu.make_async_copy(stage.at[o], out.at[pl.ds(2 * o, 2)], occ_s.at[0, 0])
    mine.start()
    for n in last:
        copies[n]().wait_send()
    mine.wait()
    for d in range(1, n_occ):
        occ_copy((o + d) % n_occ, o, d).wait_send()
        src = (o + n_occ - d) % n_occ
        occ_copy(src, src, d).wait_recv()


N_MESSAGES = 3 * NZ + (UP + DOWN) * (HALVES + NX) + 3


def on_device(integrals, occ_coeffs, virt_coeffs, block_ids, live_mask):
    blocks = integrals[0]
    n_i = occ_coeffs.shape[1]
    n_a = virt_coeffs.shape[1]
    n_occ = lax.axis_size("occ")
    bf16, f32 = jnp.bfloat16, jnp.float32
    wide = 2 * n_i
    ra, rb = CUT, ROWS - CUT
    any_space, smem = pl.BlockSpec(memory_space=pl.ANY), pl.BlockSpec(memory_space=pltpu.SMEM)
    got = pl.pallas_call(
        kernel,
        out_shape=pltpu.VMEM((2 * n_occ, n_i // n_occ, n_a), bf16),
        in_specs=[smem, smem, any_space, any_space, any_space],
        out_specs=pl.BlockSpec(memory_space=pltpu.VMEM),
        scratch_shapes=[
            *(pltpu.VMEM(((hi - lo) * NX * GROUP, *blocks.shape[1:]), bf16) for lo, hi in FIRST),
            pltpu.VMEM((OWNERS * OWNED + 1, BS, n_i), bf16),
            pltpu.VMEM((n_a, OWNERS * ROWS), bf16),
            pltpu.VMEM((NZ, NX, ROWS, wide), bf16),
            pltpu.VMEM((NZ, NX, ROWS, wide), bf16),
            pltpu.VMEM((n_a, wide), f32),
            pltpu.VMEM((n_occ, 2, n_i // n_occ, n_a), bf16),
            pltpu.VMEM((NZ, ra, wide), bf16),
            pltpu.VMEM((NZ, ra, wide), bf16),
            pltpu.VMEM((NZ, ra, wide), bf16),
            pltpu.VMEM((UP, ra, wide), bf16),
            pltpu.VMEM((DOWN, ra, wide), bf16),
            pltpu.VMEM((UP, NX, rb, wide), bf16),
            pltpu.VMEM((DOWN, NX, rb, wide), bf16),
            pltpu.VMEM((3, rb, wide), bf16),
            pltpu.SemaphoreType.DMA((2, 2 * N_MESSAGES)),
            pltpu.SemaphoreType.DMA((2, n_occ)),
            pltpu.SemaphoreType.DMA((NZ + 2,)),
        ],
        compiler_params=pltpu.CompilerParams(
            collective_id=0, has_side_effects=True, vmem_limit_bytes=63_200_000
        ),
    )(
        block_ids,
        live_mask,
        blocks,
        occ_coeffs.reshape(OWNERS * OWNED, BS, n_i),
        virt_coeffs.T,
    )
    return jnp.transpose(got, (1, 0, 2))


def solution(mesh):
    return jax.shard_map(
        on_device,
        mesh=mesh,
        in_specs=(
            P("pair", None, None, "occ"),
            P(),
            P(None, "pair"),
            P(None, "pair", None),
            P("pair", None),
        ),
        out_specs=P("occ", None, "pair"),
        check_vma=False,
    )
```
